32 devices in a mesh: seq: 16 (over z, y, core), ch: 2 (over x).
Axes of the slice: x: 2, y: 2, z: 4, core: 2. Of those that a mesh axis runs over, the one named last changes fastest.
Arguments:
- tokens: int32 [2, 32768], P(None, 'seq'), may hold values from 0 to 4
- embedding: bfloat16 [5, 256], replicated, may hold values from -6 to 6
- inner_weight: bfloat16 [256, 512], P(None, 'ch'), may hold values from -0.375 to 0.375
- gate_weight: bfloat16 [256, 512], P(None, 'ch'), may hold values from -0.375 to 0.375
- state_weight: bfloat16 [256, 32], replicated, may hold values from -0.375 to 0.375
- step_weight: bfloat16 [256, 8], P(None, 'ch'), may hold values from -0.375 to 0.375
- inner_kernel: float32 [4, 512], P(None, 'ch'), may hold values from -3 to 3
- state_kernel: float32 [4, 32], replicated, may hold values from -3 to 3
- step_bias: float32 [8], P('ch'), may hold values from -1 to 1
- decay_rates: float32 [8], P('ch'), may hold values from 3.0517578e-05 to 0.1
- skip_gain: float32 [8], P('ch'), may hold values from 0.1 to 18.5
- norm_gain: float32 [512], P('ch'), may hold values from 0.5 to 1.5
- out_weight: bfloat16 [512, 256], P('ch'), may hold values from -0.25 to 0.25
Outputs:
- mixed: bfloat16 [32768, 2, 256], P(('seq', 'ch'))
The draws below stay inside these ranges and needn't reach their ends.
All inputs are finite; a program needn't handle non-finite values.
Results may differ from the reference program's by a relative error of at most 0.012.
Values may be sent and summed in bfloat16 or wider, within the bound.
A program may use at most 128 MiB of HBM per device.

```python
import math
import jax
import jax.numpy as jnp
from jax import lax

D = 256
E = 512
NS = 16
KC = 4
BLOCK = 256
WIN = 2
H = 8
L = 32768


def draw_skip_gain(key, part):
    order_key = jax.random.fold_in(key, 11)
    jitter_key = jax.random.fold_in(key, 12)
    order = jax.random.permutation(order_key, H).astype(jnp.float32)
    level = order / max(H - 1, 1)
    lowest = 0.25
    highest = 8.0
    jitter = jax.random.uniform(jitter_key, (H,), jnp.float32, 0.85, 1.15)
    values = lowest * jnp.exp(level * jnp.log(highest / lowest)) * jitter
    return values.astype(jnp.float32)


def with_ends(values, own_key, low, high):
    place = [jax.random.randint(jax.random.fold_in(own_key, axis), (), 0, length) for axis, length in enumerate(values.shape)]
    longest = values.shape.index(max(values.shape))
    next_to = place[:longest] + [(place[longest] + 1) % values.shape[longest]] + place[longest + 1:]
    return values.at[tuple(place)].set(low).at[tuple(next_to)].set(high)


def levels(rng, extent, cuts, low, largest):
    def one(axis_at, shards_of):
        steps = jax.random.uniform(jax.random.fold_in(jax.random.fold_in(rng, 6), axis_at), (shards_of,), jnp.float32, low / len(cuts), largest / len(cuts))
        return jnp.repeat(jnp.exp(steps), extent[axis_at] // shards_of).reshape((-1,) + (1,) * (len(extent) - axis_at - 1))

    gain = one(*cuts[0])
    for cut in cuts[1:]:
        gain = gain * one(*cut)
    return gain


def noise(key, dims, scale, bound, cuts=(), kind=jnp.bfloat16):
    array = scale * jax.random.normal(key, dims, jnp.float32)
    if cuts:
        array = array * levels(key, dims, cuts, -0.22, 0.18)
    return jnp.clip(array, -bound, bound).astype(kind)


def setup_inputs(seed: int = 0) -> dict:
    splits = jax.random.split(jax.random.key(seed), 14)
    return {
        "tokens": with_ends(jax.random.randint(splits[0], (WIN, L), 0, 5), jax.random.fold_in(splits[0], 1), 0, 4).astype(jnp.int32),
        "embedding": noise(splits[1], (5, D), 1.0, 6.0),
        "inner_weight": noise(splits[2], (D, E), D ** -0.5, 0.375, ((1, 2),)),
        "gate_weight": noise(splits[3], (D, E), D ** -0.5, 0.375, ((1, 2),)),
        "state_weight": noise(splits[4], (D, 2 * NS), D ** -0.5, 0.375),
        "step_weight": noise(splits[5], (D, H), D ** -0.5, 0.375, ((1, 2),)),
        "inner_kernel": noise(splits[6], (KC, E), KC ** -0.5, 3.0, ((1, 2),), jnp.float32),
        "state_kernel": noise(splits[7], (KC, 2 * NS), KC ** -0.5, 3.0, (), jnp.float32),
        "step_bias": jnp.clip(jax.random.uniform(splits[8], (H,), jnp.float32, -1.0, 1.0) * levels(splits[8], (H,), ((0, 2),), -0.4, 0.0), -1.0, 1.0),
        "decay_rates": jnp.clip(jnp.exp(math.log(0.1) - 8.094623 * jax.random.uniform(splits[9], (H,), jnp.float32) ** levels(splits[9], (H,), ((0, 2),), -0.2, 0.2)), 3.0517578125e-05, 0.1),
        "skip_gain": draw_skip_gain(jax.random.fold_in(splits[13], 71), 0),
        "norm_gain": jnp.clip(1.0 + 0.1 * jax.random.normal(splits[11], (E,), jnp.float32), 0.5, 1.5),
        "out_weight": noise(splits[12], (E, D), E ** -0.5, 0.25, ((0, 2),)),
    }


def ssd_blocks(inner_rows, state_rows, step_sizes, decay_rates, skip_gain, block_rows):
    length, head_count = step_sizes.shape
    head_width = inner_rows.shape[-1] // head_count
    state_count = state_rows.shape[-1] // 2
    block_count = length // block_rows
    input_all = inner_rows.astype(jnp.float32).reshape(block_count, block_rows, head_count, head_width)
    key_all = state_rows[:, :state_count].astype(jnp.float32).reshape(block_count, block_rows, state_count)
    read_all = state_rows[:, state_count:].astype(jnp.float32).reshape(block_count, block_rows, state_count)
    step_all = step_sizes.reshape(block_count, block_rows, head_count)
    position = jnp.arange(block_rows)
    causal = (position[:, None] >= position[None, :])[:, :, None]

    def advance(carry_state, pieces):
        input_rows, key_rows, read_rows, step_rows = pieces
        log_decay = -step_rows * decay_rates[None, :]
        log_cumul = jnp.cumsum(log_decay, axis=0)
        read_key = jnp.dot(read_rows, key_rows.T, precision=lax.Precision.HIGHEST)
        spread = log_cumul[:, None, :] - log_cumul[None, :, :]
        kernel = jnp.where(causal, jnp.exp(jnp.where(causal, spread, 0.0)), 0.0) * read_key[:, :, None]
        driven = input_rows * step_rows[:, :, None]
        within = jnp.einsum('tsh,shp->thp', kernel, driven, precision=lax.Precision.HIGHEST)
        carried = jnp.exp(log_cumul)[:, :, None] * jnp.einsum('tn,hpn->thp', read_rows, carry_state, precision=lax.Precision.HIGHEST)
        outputs = within + carried + skip_gain[None, :, None] * input_rows
        tail_decay = jnp.exp(log_cumul[-1][None, :] - log_cumul)
        new_state = jnp.exp(log_cumul[-1])[:, None, None] * carry_state + jnp.einsum('sh,shp,sn->hpn', tail_decay, driven, key_rows, precision=lax.Precision.HIGHEST)
        return (new_state, outputs)
    zero_state = jnp.zeros((head_count, head_width, state_count), jnp.float32)
    final_state, outputs = lax.scan(advance, zero_state, (input_all, key_all, read_all, step_all))
    return (outputs.reshape(length, head_count * head_width), final_state)

def convolve(values, rim, kernel):
    extended = jnp.concatenate([rim, values], axis=-2).astype(jnp.float32)
    length = values.shape[-2]
    tap_count = kernel.shape[0]
    total = jnp.zeros(values.shape, jnp.float32)
    for offset in range(tap_count):
        begin = tap_count - 1 - offset
        total = total + kernel[offset].astype(jnp.float32) * extended[..., begin:begin + length, :]
    return jax.nn.silu(total).astype(jnp.bfloat16)

def strand_gated(strand_ids, embedding, inner_weight, gate_weight, state_weight, step_weight, inner_kernel, state_kernel, step_bias, decay_rates, skip_gain):
    embedded = embedding[strand_ids]
    inner = jnp.dot(embedded, inner_weight, preferred_element_type=jnp.float32).astype(jnp.bfloat16)
    gate = jnp.dot(embedded, gate_weight, preferred_element_type=jnp.float32).astype(jnp.bfloat16)
    state_in = jnp.dot(embedded, state_weight, preferred_element_type=jnp.float32).astype(jnp.bfloat16)
    steps = jax.nn.softplus(jnp.dot(embedded, step_weight, preferred_element_type=jnp.float32) + step_bias)
    tap_count = inner_kernel.shape[0]
    inner_conv = convolve(inner, jnp.zeros((tap_count - 1, inner.shape[1]), jnp.bfloat16), inner_kernel)
    state_conv = convolve(state_in, jnp.zeros((tap_count - 1, state_in.shape[1]), jnp.bfloat16), state_kernel)
    outputs, final_state = ssd_blocks(inner_conv, state_conv, steps, decay_rates, skip_gain, BLOCK)
    return outputs * jax.nn.silu(gate.astype(jnp.float32))

def normalize(gated, norm_gain):
    scale = lax.rsqrt(lax.optimization_barrier(jnp.mean(gated * gated, axis=-1, keepdims=True)) + 1e-05)
    return (gated * scale * norm_gain).astype(jnp.bfloat16)

def reference(tokens, embedding, inner_weight, gate_weight, state_weight, step_weight, inner_kernel, state_kernel, step_bias, decay_rates, skip_gain, norm_gain, out_weight):
    windows = []
    for window in range(WIN):
        forward_ids = tokens[window]
        complement = jnp.where(forward_ids < 4, 3 - forward_ids, 4).astype(jnp.int32)
        params = (embedding, inner_weight, gate_weight, state_weight, step_weight, inner_kernel, state_kernel, step_bias, decay_rates, skip_gain)
        normed_front = normalize(strand_gated(forward_ids, *params), norm_gain)
        normed_back = normalize(strand_gated(complement[::-1], *params), norm_gain)[::-1]
        result = jnp.dot(normed_front, out_weight, preferred_element_type=jnp.float32) + jnp.dot(normed_back, out_weight, preferred_element_type=jnp.float32)
        windows.append(result.astype(jnp.bfloat16))
    return jnp.stack(windows, axis=1)
```

```python
from functools import partial

import jax
import jax.numpy as jnp
import numpy as np
from jax import lax
from jax.experimental import pallas as pl
from jax.experimental.pallas import tpu as pltpu
from jax.sharding import PartitionSpec as P

SUB = 64
ROWS = 256
EPS = 1e-05
COLS = 128


def split3(v):
    hi = lax.reduce_precision(v, 8, 7)
    rest = v - hi
    mid = lax.reduce_precision(rest, 8, 7)
    low = lax.reduce_precision(rest - mid, 8, 7)
    return hi, mid, low


def pieces(table):
    taps, ids, width = table.shape
    full = jnp.pad(table, ((0, 4 - taps), (0, 8 - ids), (0, 0))).reshape(32, width)
    stacked = jnp.concatenate(split3(full) + (jnp.zeros_like(full),), axis=0)
    return stacked.astype(jnp.bfloat16)


def silu(v):
    return v * (1.0 / (1.0 + jnp.exp(-v)))


def dot(a, b):
    return jnp.dot(a, b, preferred_element_type=jnp.float32)


def state_kernel_body(oh_ref, tri_ref, tx_ref, tst_ref, tdt_ref, ld_ref, x_ref, kv_ref, sloc_ref, sfin_ref):
    @pl.when(pl.program_id(1) == 0)
    def _():
        sfin_ref[...] = jnp.zeros_like(sfin_ref)

    oh = oh_ref[0]
    x = silu(dot(oh, tx_ref[...])).astype(jnp.bfloat16)
    x_ref[0] = x
    kv = silu(dot(oh, tst_ref[...])).astype(jnp.bfloat16)
    kv_ref[0] = kv
    cum = dot(dot(tri_ref[...], oh).astype(jnp.bfloat16), ld_ref[...])
    dt = dot(oh, tdt_ref[...])
    state = sfin_ref[0]
    for j in range(ROWS // SUB):
        rows = slice(j * SUB, (j + 1) * SUB)
        cum_j = cum[rows]
        tot = cum_j[SUB - 1 :]
        wx = (x[rows].astype(jnp.float32) * dt[rows] * jnp.exp(tot - cum_j)).astype(jnp.bfloat16)
        new = lax.dot_general(
            kv[rows, :16], wx, (((0,), (0,)), ((), ())), preferred_element_type=jnp.float32
        )
        sloc_ref[0, j] = new
        state = jnp.exp(tot) * state + new
    sfin_ref[0] = state


def output_kernel_body(
    oh_ref, x_ref, kv_ref, sloc_ref, inc_ref, tri_ref, tdt_ref, tsg_ref, ld_ref,
    skip_ref, gain_ref, ow_ref, causal_ref, diag_ref, bd_ref, flip_ref,
    out_ref, state_ref, front_ref,
):
    strand, sb = pl.program_id(1), pl.program_id(2)
    count = pl.num_programs(2)

    @pl.when(sb == 0)
    def _():
        state_ref[...] = inc_ref[0]

    oh = oh_ref[0]
    cum = dot(dot(tri_ref[...], oh).astype(jnp.bfloat16), ld_ref[...])
    dt = dot(oh, tdt_ref[...])
    sg = dot(oh, tsg_ref[...])
    skip, gain = skip_ref[...], gain_ref[...]
    causal, diag, bd = causal_ref[...], diag_ref[...], bd_ref[...]
    state = state_ref[...]
    parts = []
    for j in range(ROWS // SUB):
        rows = slice(j * SUB, (j + 1) * SUB)
        cum_j = cum[rows]
        tot = cum_j[SUB - 1 :]
        xj = x_ref[0, rows, :].astype(jnp.float32)
        driven = (xj * dt[rows]).astype(jnp.bfloat16)
        key, read = kv_ref[0, rows, :16], kv_ref[0, rows, 16:32]
        crow = jnp.sum(cum_j * diag, axis=0, keepdims=True)
        rk = lax.dot_general(
            read, jnp.concatenate([key, key], axis=0), (((1,), (1,)), ((), ())),
            preferred_element_type=jnp.float32,
        )
        rk = jnp.concatenate([rk] * 4, axis=1)
        kmat = (jnp.exp(jnp.minimum(cum_j - crow, 0.0)) * causal * rk).astype(jnp.bfloat16)
        within = []
        for g in range(2):
            lanes = slice(g * 256, (g + 1) * 256)
            rhs = jnp.concatenate([driven[:, lanes]] * 4, axis=0) * bd
            within.append(dot(kmat[:, lanes], rhs))
        carried = jnp.exp(cum_j) * dot(read, state.astype(jnp.bfloat16))
        y = jnp.concatenate(within, axis=1) + carried + skip * xj
        state = jnp.exp(tot) * state + sloc_ref[0, j]
        gated = y * sg[rows]
        mean = jnp.mean(gated * gated, axis=-1, keepdims=True)
        parts.append((gated * lax.rsqrt(mean + EPS) * gain).astype(jnp.bfloat16))
    state_ref[...] = state
    normed = jnp.concatenate(parts, axis=0)

    @pl.when(strand == 0)
    def _():
        front_ref[pl.ds(pl.multiple_of(sb * ROWS, ROWS), ROWS), :] = normed

    @pl.when(strand == 1)
    def _():
        back = dot(flip_ref[...], normed).astype(jnp.bfloat16)
        start = pl.multiple_of((count - 1 - sb) * ROWS, ROWS)
        front = front_ref[pl.ds(start, ROWS), :]
        ow = ow_ref[...]
        out_ref[...] = (dot(front, ow) + dot(back, ow)).astype(out_ref.dtype)


def whole_spec(array):
    return pl.BlockSpec(array.shape, lambda *_: (0,) * array.ndim)


def on_device(
    tokens, embedding, inner_weight, gate_weight, state_weight, step_weight, inner_kernel,
    state_kernel, step_bias, decay_rates, skip_gain, norm_gain, out_weight,
):
    f32, bf16 = jnp.float32, jnp.bfloat16
    wins, held = tokens.shape
    chs, seqs = lax.axis_size("ch"), lax.axis_size("seq")
    ch, seq = lax.axis_index("ch"), lax.axis_index("seq")
    rows = held // chs
    devices = seqs * chs
    me = seq * chs + ch
    heads_here = decay_rates.shape[0]
    width = inner_weight.shape[1]
    head_width = width // heads_here

    inner_tab = dot(embedding, inner_weight).astype(bf16).astype(f32)
    gate_tab = dot(embedding, gate_weight).astype(bf16).astype(f32)
    state_tab = dot(embedding, state_weight).astype(bf16).astype(f32)
    step_tab = jax.nn.softplus(dot(embedding, step_weight) + step_bias)
    spread = lambda v: jnp.repeat(v, head_width, axis=-1)
    packed = jnp.concatenate(
        [
            inner_tab,
            jax.nn.silu(gate_tab),
            spread(step_tab),
            spread(-step_tab * decay_rates),
            inner_kernel,
            spread(skip_gain)[None],
            norm_gain[None],
        ],
        axis=0,
    )
    packed = lax.all_gather(packed, "ch", axis=1, tiled=True)
    ow = lax.all_gather(out_weight, "ch", axis=0, tiled=True)
    inner_all, sg_all, step_all, ld_all = (packed[5 * i : 5 * i + 5] for i in range(4))
    taps_all, skip_all, gain_all = packed[20:24], packed[24:25], packed[25:26]
    tx = pieces(taps_all[:, None, :] * inner_all[None])
    tst = pieces(jnp.pad(state_kernel[:, None, :] * state_tab[None], ((0, 0), (0, 0), (0, 96))))
    tdt, tsg, ld = pieces(step_all[None]), pieces(sg_all[None]), pieces(ld_all[None])

    halves = tokens.reshape(wins, chs, rows)
    base = jnp.arange(5, dtype=jnp.int32)
    counts = jnp.sum((halves[..., None] == base).astype(jnp.int32), axis=2)
    info = jnp.concatenate(
        [counts.reshape(wins, chs * 5), tokens[:, :3], tokens[:, held - 3 :]], axis=1
    )
    info = lax.all_gather(info, "seq")
    none = 7
    edge = info[:, :, chs * 5 :]
    before = jnp.where(seq > 0, edge[jnp.maximum(seq - 1, 0)][:, 3:], none)
    after = jnp.where(seq < seqs - 1, edge[jnp.minimum(seq + 1, seqs - 1)][:, :3], none)
    around = jnp.concatenate([before, tokens, after], axis=1)
    mine = lax.dynamic_slice_in_dim(around, ch * rows, rows + 6, axis=1)
    other = jnp.where(mine < 4, 3 - mine, mine)[:, ::-1]
    ids = jnp.stack([mine, other], axis=1).reshape(wins * 2, rows + 6)
    column = np.arange(COLS)
    tap_of, id_of = (column // 8) % 4, column % 8
    onehot = jnp.zeros((wins * 2, rows, COLS), jnp.bool_)
    for k in range(4):
        tap = ids[:, 3 - k : 3 - k + rows, None] == jnp.asarray(id_of, jnp.int32)
        onehot = onehot | (tap & jnp.asarray(tap_of == k))
    onehot = onehot.astype(bf16)

    streams, steps = wins * 2, rows // ROWS
    subs = ROWS // SUB
    full = width * chs
    index = np.arange(ROWS)
    tri = jnp.asarray(
        (index[:, None] >= index[None]) & (index[:, None] // SUB == index[None] // SUB), bf16
    )
    row_spec = lambda n: pl.BlockSpec((1, ROWS, n), lambda s, b: (s, b, 0))
    x, kv, sloc, sfin = pl.pallas_call(
        state_kernel_body,
        grid=(streams, steps),
        in_specs=[row_spec(COLS)] + [whole_spec(v) for v in (tri, tx, tst, tdt, ld)],
        out_specs=[
            row_spec(full),
            row_spec(128),
            pl.BlockSpec((1, subs, 16, full), lambda s, b: (s, b, 0, 0)),
            pl.BlockSpec((1, 16, full), lambda s, b: (s, 0, 0)),
        ],
        out_shape=[
            jax.ShapeDtypeStruct((streams, rows, full), bf16),
            jax.ShapeDtypeStruct((streams, rows, 128), bf16),
            jax.ShapeDtypeStruct((streams, steps * subs, 16, full), f32),
            jax.ShapeDtypeStruct((streams, 16, full), f32),
        ],
        compiler_params=pltpu.CompilerParams(vmem_limit_bytes=40 << 20),
        name="states",
    )(onehot, tri, tx, tst, tdt, ld)

    gathered = lax.all_gather(sfin.astype(bf16), ("seq", "ch"))
    every = info[:, :, : chs * 5].reshape(seqs, wins, chs, 5)
    every = jnp.moveaxis(every, 2, 1).reshape(devices, wins, 5).astype(f32)
    j, m = np.arange(devices)[:, None], np.arange(devices)[None]
    fwd = (j < m) & (m < me)
    bwd = (j > m) & (m > me)
    between = jnp.stack(
        [
            jnp.sum(jnp.where(fwd[..., None, None], every[None], 0.0), axis=1),
            jnp.sum(jnp.where(bwd[..., None, None], every[None][..., jnp.array([3, 2, 1, 0, 4])], 0.0), axis=1),
        ],
        axis=2,
    )
    log_weight = jnp.sum(between[..., None] * ld_all, axis=3)
    who = np.arange(devices)
    reached = jnp.stack([who < me, who > me], axis=1)[:, None, :, None]
    weight = jnp.where(reached, jnp.exp(log_weight), 0.0).reshape(devices, streams, 1, full)
    incoming = jnp.sum(weight * gathered.astype(f32), axis=0)

    lane, t = np.arange(full)[None], np.arange(SUB)[:, None]
    causal = jnp.asarray(t >= lane % SUB, f32)
    diag = jnp.asarray(t == lane % SUB, f32)
    bd = jnp.asarray(np.arange(256)[:, None] // 64 == np.arange(256)[None] // 64, bf16)
    flip = jnp.asarray(np.eye(ROWS)[::-1], bf16)
    stream = lambda shape: pl.BlockSpec(
        (1,) + shape, lambda w, s, b: (w * 2 + s, b) + (0,) * (len(shape) - 1)
    )
    consts = (tri, tdt, tsg, ld, skip_all, gain_all, ow, causal, diag, bd, flip)
    model = out_weight.shape[1]
    out = pl.pallas_call(
        output_kernel_body,
        grid=(wins, 2, steps),
        in_specs=[
            stream((ROWS, COLS)),
            stream((ROWS, full)),
            stream((ROWS, 128)),
            stream((subs, 16, full)),
            pl.BlockSpec((1, 16, full), lambda w, s, b: (w * 2 + s, 0, 0)),
        ]
        + [whole_spec(v) for v in consts],
        out_specs=pl.BlockSpec((ROWS, model), lambda w, s, b: (steps - 1 - b * s, w)),
        out_shape=jax.ShapeDtypeStruct((rows, wins * model), bf16),
        scratch_shapes=[pltpu.VMEM((16, full), f32), pltpu.VMEM((rows, full), bf16)],
        compiler_params=pltpu.CompilerParams(vmem_limit_bytes=40 << 20),
        name="outputs",
    )(onehot, x, kv, sloc, incoming, *consts)
    return out.reshape(rows, wins, model)


def solution(mesh):
    placed = (
        P(None, "seq"), P(), P(None, "ch"), P(None, "ch"), P(), P(None, "ch"), P(None, "ch"), P(),
        P("ch"), P("ch"), P("ch"), P("ch"), P("ch", None),
    )
    return jax.shard_map(
        on_device,
        mesh=mesh,
        in_specs=placed,
        out_specs=P(("seq", "ch"), None, None),
        check_vma=False,
    )
```

```python
from functools import partial

import jax
import jax.numpy as jnp
import numpy as np
from jax import lax
from jax.experimental import pallas as pl
from jax.experimental.pallas import tpu as pltpu
from jax.sharding import PartitionSpec as P

SUB = 64
ROWS = 256
EPS = 1e-05
COLS = 128


def split3(v):
    hi = lax.reduce_precision(v, 8, 7)
    rest = v - hi
    mid = lax.reduce_precision(rest, 8, 7)
    low = lax.reduce_precision(rest - mid, 8, 7)
    return hi, mid, low


def pieces(table):
    taps, ids, width = table.shape
    full = jnp.pad(table, ((0, 4 - taps), (0, 8 - ids), (0, 0))).reshape(32, width)
    stacked = jnp.concatenate(split3(full) + (jnp.zeros_like(full),), axis=0)
    return stacked.astype(jnp.bfloat16)


def silu(v):
    return v * (1.0 / (1.0 + jnp.exp(-v)))


def dot(a, b):
    return jnp.dot(a, b, preferred_element_type=jnp.float32)


def state_kernel_body(oh_ref, tri_ref, tx_ref, tst_ref, tdt_ref, ld_ref, x_ref, kv_ref, sloc_ref, sfin_ref, state_ref):
    @pl.when(pl.program_id(1) == 0)
    def _():
        state_ref[...] = jnp.zeros_like(state_ref)

    oh = oh_ref[0]
    x = silu(dot(oh, tx_ref[...])).astype(jnp.bfloat16)
    x_ref[0] = x
    kv = silu(dot(oh, tst_ref[...])).astype(jnp.bfloat16)
    kv_ref[0] = kv
    cum = dot(dot(tri_ref[...], oh).astype(jnp.bfloat16), ld_ref[...])
    dt = dot(oh, tdt_ref[...])
    state = state_ref[...]
    for j in range(ROWS // SUB):
        rows = slice(j * SUB, (j + 1) * SUB)
        cum_j = cum[rows]
        tot = cum_j[SUB - 1 :]
        wx = (x[rows].astype(jnp.float32) * dt[rows] * jnp.exp(tot - cum_j)).astype(jnp.bfloat16)
        new = lax.dot_general(
            kv[rows, :16], wx, (((0,), (0,)), ((), ())), preferred_element_type=jnp.float32
        )
        sloc_ref[0, j] = new
        state = jnp.exp(tot) * state + new
    state_ref[...] = state
    half = state.shape[1] // 2
    sfin_ref[0] = state[:, :half].astype(jnp.bfloat16)
    sfin_ref[1] = state[:, half:].astype(jnp.bfloat16)


def output_kernel_body(
    oh_ref, x_ref, kv_ref, sloc_ref, inc_ref, tri_ref, tdt_ref, tsg_ref, ld_ref,
    skip_ref, gain_ref, ow_ref, causal_ref, diag_ref, bd_ref, flip_ref,
    out_ref, state_ref, front_ref,
):
    strand, sb = pl.program_id(1), pl.program_id(2)
    count = pl.num_programs(2)

    @pl.when(sb == 0)
    def _():
        state_ref[...] = jnp.concatenate([inc_ref[0], inc_ref[1]], axis=1).astype(jnp.float32)

    oh = oh_ref[0]
    cum = dot(dot(tri_ref[...], oh).astype(jnp.bfloat16), ld_ref[...])
    dt = dot(oh, tdt_ref[...])
    sg = dot(oh, tsg_ref[...])
    skip, gain = skip_ref[...], gain_ref[...]
    causal, diag, bd = causal_ref[...], diag_ref[...], bd_ref[...]
    state = state_ref[...]
    parts = []
    for j in range(ROWS // SUB):
        rows = slice(j * SUB, (j + 1) * SUB)
        cum_j = cum[rows]
        tot = cum_j[SUB - 1 :]
        xj = x_ref[0, rows, :].astype(jnp.float32)
        driven = (xj * dt[rows]).astype(jnp.bfloat16)
        key, read = kv_ref[0, rows, :16], kv_ref[0, rows, 16:32]
        crow = jnp.sum(cum_j * diag, axis=0, keepdims=True)
        rk = lax.dot_general(
            read, jnp.concatenate([key, key], axis=0), (((1,), (1,)), ((), ())),
            preferred_element_type=jnp.float32,
        )
        rk = jnp.concatenate([rk] * 4, axis=1)
        kmat = (jnp.exp(jnp.minimum(cum_j - crow, 0.0)) * causal * rk).astype(jnp.bfloat16)
        within = []
        for g in range(2):
            lanes = slice(g * 256, (g + 1) * 256)
            rhs = jnp.concatenate([driven[:, lanes]] * 4, axis=0) * bd
            within.append(dot(kmat[:, lanes], rhs))
        carried = jnp.exp(cum_j) * dot(read, state.astype(jnp.bfloat16))
        y = jnp.concatenate(within, axis=1) + carried + skip * xj
        state = jnp.exp(tot) * state + sloc_ref[0, j]
        gated = y * sg[rows]
        mean = jnp.mean(gated * gated, axis=-1, keepdims=True)
        parts.append((gated * lax.rsqrt(mean + EPS) * gain).astype(jnp.bfloat16))
    state_ref[...] = state
    normed = jnp.concatenate(parts, axis=0)

    @pl.when(strand == 0)
    def _():
        front_ref[pl.ds(pl.multiple_of(sb * ROWS, ROWS), ROWS), :] = normed

    @pl.when(strand == 1)
    def _():
        back = dot(flip_ref[...], normed).astype(jnp.bfloat16)
        start = pl.multiple_of((count - 1 - sb) * ROWS, ROWS)
        front = front_ref[pl.ds(start, ROWS), :]
        ow = ow_ref[...]
        out_ref[...] = (dot(front, ow) + dot(back, ow)).astype(out_ref.dtype)


MESH = pl.DeviceIdType.MESH
GROUP = 8


def exchange_body(
    chs, devices, info_ref, packed_ref, ow_ref, info_out, packed_out, ow_out,
    info_all, packed_all, ow_all, send, recv, psend, precv, osend, orecv,
):
    seq, ch = lax.axis_index("seq"), lax.axis_index("ch")
    me = seq * chs + ch
    place = lambda d: (d // chs, lax.rem(d, chs))
    barrier = pltpu.get_barrier_semaphore()

    def greet(d, _):
        pl.semaphore_signal(
            barrier, inc=1, device_id=place(lax.rem(me + d, devices)), device_id_type=MESH
        )
        return 0

    lax.fori_loop(1, devices, greet, 0)
    pl.semaphore_wait(barrier, devices - 1)

    def remote(src, dst, ssem, rsem, device):
        return pltpu.make_async_remote_copy(
            src_ref=src, dst_ref=dst, send_sem=ssem, recv_sem=rsem, device_id=device,
            device_id_type=MESH,
        )

    def info_copy(d, slot):
        return remote(
            info_ref, info_all.at[slot], send.at[d], recv.at[d], place(lax.rem(me + d, devices))
        )

    def start(d, _):
        info_copy(d, me).start()
        return 0

    def finish(d, _):
        info_copy(d, lax.rem(me + devices - d, devices)).wait()
        return 0

    def table_copies(d, slot):
        device = (seq, lax.rem(ch + d, chs))
        return (
            remote(packed_ref, packed_all.at[slot], psend.at[d], precv.at[d], device),
            remote(ow_ref, ow_all.at[slot], osend.at[d], orecv.at[d], device),
        )

    for d in range(1, chs):
        for copy in table_copies(d, ch):
            copy.start()
    lax.fori_loop(1, devices, start, 0)
    info_all[me] = info_ref[...]
    packed_all[ch] = packed_ref[...]
    ow_all[ch] = ow_ref[...]
    for d in range(1, chs):
        for copy in table_copies(d, lax.rem(ch + chs - d, chs)):
            copy.wait()
    lax.fori_loop(1, devices, finish, 0)
    info_out[...] = info_all[...]
    packed_out[...] = packed_all[...]
    ow_out[...] = ow_all[...]


def carry_body(
    chs, groups, s_ref, log_ref, out_ref, first, total, second, third, landed,
    send1, recv1, send2, recv2, send3, recv3,
):
    me = lax.axis_index("seq") * chs + lax.axis_index("ch")
    g, q = me // GROUP, lax.rem(me, GROUP)
    strand = lax.rem(q // 2, 2)
    place = lambda d: (d // chs, lax.rem(d, chs))
    mate = lambda d: place(g * GROUP + lax.rem(q + d, GROUP))
    peer = lambda d: place(lax.rem(g + d, groups) * GROUP + q)
    barrier = pltpu.get_barrier_semaphore()
    for d in range(1, GROUP):
        pl.semaphore_signal(barrier, inc=1, device_id=mate(d), device_id_type=MESH)

    def greet(d, _):
        pl.semaphore_signal(barrier, inc=1, device_id=peer(d), device_id_type=MESH)
        return 0

    lax.fori_loop(1, groups, greet, 0)
    pl.semaphore_wait(barrier, GROUP - 1 + groups - 1)

    def remote(src, dst, ssem, rsem, device):
        return pltpu.make_async_remote_copy(
            src_ref=src, dst_ref=dst, send_sem=ssem, recv_sem=rsem, device_id=device,
            device_id_type=MESH,
        )

    def within(source, target, ssem, rsem, d, slot):
        return remote(source.at[lax.rem(q + d, GROUP)], target.at[slot], ssem.at[d], rsem.at[d], mate(d))

    def swap(source, target, ssem, rsem):
        for d in range(1, GROUP):
            within(source, target, ssem, rsem, d, q).start()
        target[q] = source[q]
        for d in range(1, GROUP):
            within(source, target, ssem, rsem, d, lax.rem(q + GROUP - d, GROUP)).wait()

    swap(s_ref, first, send1, recv1)
    f32, bf16 = jnp.float32, jnp.bfloat16
    zero = jnp.zeros(total.shape, f32)
    member = lambda k: k + strand * (GROUP - 1 - 2 * k)
    grow = [jnp.exp(log_ref[g * GROUP + member(k)]) for k in range(GROUP)]
    added = [first[member(k)].astype(f32) for k in range(GROUP)]
    state = zero
    for k in range(GROUP):
        state = grow[k] * state + added[k]
    total[...] = state.astype(bf16)

    def across(d, slot):
        return remote(total, second.at[slot], send2.at[d], recv2.at[d], peer(d))

    def start(d, _):
        across(d, g).start()
        return 0

    def finish(d, _):
        across(d, lax.rem(g + groups - d, groups)).wait()
        return 0

    lax.fori_loop(1, groups, start, 0)
    second[g] = total[...]
    lax.fori_loop(1, groups, finish, 0)
    order = g + strand * (groups - 1 - 2 * g)

    def earlier(k, state):
        at = k + strand * (groups - 1 - 2 * k)
        logs = log_ref[at * GROUP]
        for i in range(1, GROUP):
            logs = logs + log_ref[at * GROUP + i]
        new = jnp.exp(logs) * state + second[at].astype(f32)
        return jnp.where(k < order, new, state)

    state = lax.fori_loop(0, groups, earlier, zero)
    for k in range(GROUP):
        third[member(k)] = state.astype(bf16)
        state = grow[k] * state + added[k]
    swap(third, landed, send3, recv3)
    out_ref[...] = landed[...]


def whole_spec(array):
    return pl.BlockSpec(array.shape, lambda *_: (0,) * array.ndim)


def on_device(
    tokens, embedding, inner_weight, gate_weight, state_weight, step_weight, inner_kernel,
    state_kernel, step_bias, decay_rates, skip_gain, norm_gain, out_weight,
):
    f32, bf16 = jnp.float32, jnp.bfloat16
    wins, held = tokens.shape
    chs, seqs = lax.axis_size("ch"), lax.axis_size("seq")
    ch, seq = lax.axis_index("ch"), lax.axis_index("seq")
    rows = held // chs
    devices = seqs * chs
    me = seq * chs + ch
    heads_here = decay_rates.shape[0]
    width = inner_weight.shape[1]
    head_width = width // heads_here

    inner_tab = dot(embedding, inner_weight).astype(bf16).astype(f32)
    gate_tab = dot(embedding, gate_weight).astype(bf16).astype(f32)
    state_tab = dot(embedding, state_weight).astype(bf16).astype(f32)
    step_tab = jax.nn.softplus(dot(embedding, step_weight) + step_bias)
    spread = lambda v: jnp.repeat(v, head_width, axis=-1)
    packed = jnp.concatenate(
        [
            inner_tab,
            jax.nn.silu(gate_tab),
            spread(step_tab),
            spread(-step_tab * decay_rates),
            inner_kernel,
            spread(skip_gain)[None],
            norm_gain[None],
        ],
        axis=0,
    )
    packed = jnp.pad(packed, ((0, 32 - packed.shape[0]), (0, 0)))

    mine = lax.dynamic_slice_in_dim(tokens, ch * rows, rows, axis=1)
    base = jnp.arange(5, dtype=jnp.int32)
    counts = jnp.sum((mine[..., None] == base).astype(jnp.int32), axis=1)
    info = jnp.concatenate([counts, mine[:, :3], mine[:, rows - 3 :]], axis=1)
    info = jnp.pad(info, ((0, 8 - wins), (0, 128 - info.shape[1])))
    vmem = pl.BlockSpec(memory_space=pltpu.VMEM)
    dma = pltpu.SemaphoreType.DMA
    tables = [
        jax.ShapeDtypeStruct((devices,) + info.shape, jnp.int32),
        jax.ShapeDtypeStruct((chs,) + packed.shape, f32),
        jax.ShapeDtypeStruct((chs,) + out_weight.shape, bf16),
    ]
    info, packed, ow = pl.pallas_call(
        partial(exchange_body, chs, devices),
        in_specs=[vmem] * 3,
        out_specs=[vmem] * 3,
        out_shape=tables,
        scratch_shapes=[pltpu.VMEM(v.shape, v.dtype) for v in tables]
        + [dma((devices,))] * 2 + [dma((chs,))] * 4,
        compiler_params=pltpu.CompilerParams(collective_id=0, has_side_effects=True),
        name="exchange",
    )(info, packed, out_weight)
    packed = jnp.concatenate([packed[i] for i in range(chs)], axis=1)
    ow = ow.reshape(chs * width, -1)
    inner_all, sg_all, step_all, ld_all = (packed[5 * i : 5 * i + 5] for i in range(4))
    taps_all, skip_all, gain_all = packed[20:24], packed[24:25], packed[25:26]
    tx = pieces(taps_all[:, None, :] * inner_all[None])
    tst = pieces(jnp.pad(state_kernel[:, None, :] * state_tab[None], ((0, 0), (0, 0), (0, 96))))
    tdt, tsg, ld = pieces(step_all[None]), pieces(sg_all[None]), pieces(ld_all[None])

    none = 7
    before = jnp.where(me > 0, info[jnp.maximum(me - 1, 0), :wins, 8:11], none)
    after = jnp.where(me < devices - 1, info[jnp.minimum(me + 1, devices - 1), :wins, 5:8], none)
    mine = jnp.concatenate([before, mine, after], axis=1)
    other = jnp.where(mine < 4, 3 - mine, mine)[:, ::-1]
    ids = jnp.stack([mine, other], axis=1).reshape(wins * 2, rows + 6)
    column = np.arange(COLS)
    tap_of, id_of = (column // 8) % 4, column % 8
    onehot = jnp.zeros((wins * 2, rows, COLS), jnp.bool_)
    for k in range(4):
        tap = ids[:, 3 - k : 3 - k + rows, None] == jnp.asarray(id_of, jnp.int32)
        onehot = onehot | (tap & jnp.asarray(tap_of == k))
    onehot = onehot.astype(bf16)

    streams, steps = wins * 2, rows // ROWS
    subs = ROWS // SUB
    full = width * chs
    index = np.arange(ROWS)
    tri = jnp.asarray(
        (index[:, None] >= index[None]) & (index[:, None] // SUB == index[None] // SUB), bf16
    )
    row_spec = lambda n: pl.BlockSpec((1, ROWS, n), lambda s, b: (s, b, 0))
    x, kv, sloc, sfin = pl.pallas_call(
        state_kernel_body,
        grid=(streams, steps),
        in_specs=[row_spec(COLS)] + [whole_spec(v) for v in (tri, tx, tst, tdt, ld)],
        out_specs=[
            row_spec(full),
            row_spec(128),
            pl.BlockSpec((1, subs, 16, full), lambda s, b: (s, b, 0, 0)),
            pl.BlockSpec((2, 16, full // 2), lambda s, b: (s, 0, 0)),
        ],
        out_shape=[
            jax.ShapeDtypeStruct((streams, rows, full), bf16),
            jax.ShapeDtypeStruct((streams, rows, 128), bf16),
            jax.ShapeDtypeStruct((streams, steps * subs, 16, full), f32),
            jax.ShapeDtypeStruct((streams * 2, 16, full // 2), bf16),
        ],
        scratch_shapes=[pltpu.VMEM((16, full), f32)],
        compiler_params=pltpu.CompilerParams(vmem_limit_bytes=56 << 20),
        name="states",
    )(onehot, tri, tx, tst, tdt, ld)

    q = lax.rem(me, GROUP)
    window, strand, half = q // 4, (q // 2) % 2, q % 2
    cnt = info[:, window, :5]
    cnt = jnp.where(strand == 0, cnt, jnp.stack([cnt[:, i] for i in (3, 2, 1, 0, 4)], axis=1))
    part = full // 2
    ld_half = lax.dynamic_slice_in_dim(ld_all, half * part, part, axis=1)
    logs = jnp.sum(cnt.astype(f32)[:, :, None] * ld_half[None], axis=1)[:, None, :]
    groups = devices // GROUP
    piece = (16, part)
    incoming = pl.pallas_call(
        partial(carry_body, chs, groups),
        in_specs=[vmem] * 2,
        out_specs=vmem,
        out_shape=jax.ShapeDtypeStruct((GROUP,) + piece, bf16),
        scratch_shapes=[
            pltpu.VMEM((GROUP,) + piece, bf16),
            pltpu.VMEM(piece, bf16),
            pltpu.VMEM((groups,) + piece, bf16),
            pltpu.VMEM((GROUP,) + piece, bf16),
            pltpu.VMEM((GROUP,) + piece, bf16),
        ]
        + [dma((GROUP,))] * 2 + [dma((groups,))] * 2 + [dma((GROUP,))] * 2,
        compiler_params=pltpu.CompilerParams(collective_id=1, has_side_effects=True),
        name="carry",
    )(sfin, logs)

    lane, t = np.arange(full)[None], np.arange(SUB)[:, None]
    causal = jnp.asarray(t >= lane % SUB, f32)
    diag = jnp.asarray(t == lane % SUB, f32)
    bd = jnp.asarray(np.arange(256)[:, None] // 64 == np.arange(256)[None] // 64, bf16)
    flip = jnp.asarray(np.eye(ROWS)[::-1], bf16)
    stream = lambda shape: pl.BlockSpec(
        (1,) + shape, lambda w, s, b: (w * 2 + s, b) + (0,) * (len(shape) - 1)
    )
    consts = (tri, tdt, tsg, ld, skip_all, gain_all, ow, causal, diag, bd, flip)
    model = out_weight.shape[1]
    out = pl.pallas_call(
        output_kernel_body,
        grid=(wins, 2, steps),
        in_specs=[
            stream((ROWS, COLS)),
            stream((ROWS, full)),
            stream((ROWS, 128)),
            stream((subs, 16, full)),
            pl.BlockSpec((2, 16, full // 2), lambda w, s, b: (w * 2 + s, 0, 0)),
        ]
        + [whole_spec(v) for v in consts],
        out_specs=pl.BlockSpec((ROWS, model), lambda w, s, b: (steps - 1 - b * s, w)),
        out_shape=jax.ShapeDtypeStruct((rows, wins * model), bf16),
        scratch_shapes=[pltpu.VMEM((16, full), f32), pltpu.VMEM((rows, full), bf16)],
        compiler_params=pltpu.CompilerParams(vmem_limit_bytes=56 << 20),
        name="outputs",
    )(onehot, x, kv, sloc, incoming, *consts)
    return out.reshape(rows, wins, model)


def solution(mesh):
    placed = (
        P(None, "seq"), P(), P(None, "ch"), P(None, "ch"), P(), P(None, "ch"), P(None, "ch"), P(),
        P("ch"), P("ch"), P("ch"), P("ch"), P("ch", None),
    )
    return jax.shard_map(
        on_device,
        mesh=mesh,
        in_specs=placed,
        out_specs=P(("seq", "ch"), None, None),
        check_vma=False,
    )
```

```python
from functools import partial

import jax
import jax.numpy as jnp
import numpy as np
from jax import lax
from jax.experimental import pallas as pl
from jax.experimental.pallas import tpu as pltpu
from jax.sharding import PartitionSpec as P

SUB = 64
ROWS = 256
EPS = 1e-05
COLS = 128


def silu(v):
    return v * (1.0 / (1.0 + jnp.exp(-v)))


def dot(a, b):
    return jnp.dot(a, b, preferred_element_type=jnp.float32)


def state_kernel_body(oh_ref, tri_ref, tx_ref, tst_ref, tdt_ref, ld_ref, x_ref, kv_ref, sloc_ref, sfin_ref, state_ref, log_ref):
    @pl.when(pl.program_id(1) == 0)
    def _():
        state_ref[...] = jnp.zeros_like(state_ref)
        log_ref[...] = jnp.zeros_like(log_ref)

    oh = oh_ref[0]
    x = silu(dot(oh, tx_ref[...])).astype(jnp.bfloat16)
    x_ref[0] = x
    kv = silu(dot(oh, tst_ref[...])).astype(jnp.bfloat16)
    kv_ref[0] = kv
    cum = dot(dot(tri_ref[...], oh).astype(jnp.bfloat16), ld_ref[...])
    dt = dot(oh, tdt_ref[...])
    state, log = state_ref[...], log_ref[...]
    for j in range(ROWS // SUB):
        rows = slice(j * SUB, (j + 1) * SUB)
        cum_j = cum[rows]
        tot = cum_j[SUB - 1 :]
        log = log + tot
        wx = (x[rows].astype(jnp.float32) * dt[rows] * jnp.exp(tot - cum_j)).astype(jnp.bfloat16)
        new = lax.dot_general(
            kv[rows, :16], wx, (((0,), (0,)), ((), ())), preferred_element_type=jnp.float32
        )
        sloc_ref[0, j] = new
        state = jnp.exp(tot) * state + new
    state_ref[...] = state
    half = state.shape[1] // 2
    log_ref[...] = log
    for i in range(2):
        lanes = slice(i * half, (i + 1) * half)
        sfin_ref[i, 0:16, :] = state[:, lanes]
        sfin_ref[i, 16:24, :] = jnp.broadcast_to(log[:, lanes], (8, half))


def output_kernel_body(
    oh_ref, x_ref, kv_ref, sloc_ref, inc_ref, tri_ref, tdt_ref, tsg_ref, ld_ref,
    skip_ref, gain_ref, ow_ref, causal_ref, diag_ref, bd_ref, flip_ref,
    out_ref, state_ref, front_ref,
):
    strand, sb = pl.program_id(1), pl.program_id(2)
    count = pl.num_programs(2)

    @pl.when(sb == 0)
    def _():
        state_ref[...] = jnp.concatenate([inc_ref[0], inc_ref[1]], axis=1).astype(jnp.float32)

    oh = oh_ref[0]
    cum = dot(dot(tri_ref[...], oh).astype(jnp.bfloat16), ld_ref[...])
    dt = dot(oh, tdt_ref[...])
    sg = dot(oh, tsg_ref[...])
    skip, gain = skip_ref[...], gain_ref[...]
    causal, diag, bd = causal_ref[...], diag_ref[...], bd_ref[...]
    state = state_ref[...]
    parts = []
    for j in range(ROWS // SUB):
        rows = slice(j * SUB, (j + 1) * SUB)
        cum_j = cum[rows]
        tot = cum_j[SUB - 1 :]
        xj = x_ref[0, rows, :].astype(jnp.float32)
        driven = (xj * dt[rows]).astype(jnp.bfloat16)
        key, read = kv_ref[0, rows, :16], kv_ref[0, rows, 16:32]
        crow = jnp.sum(cum_j * diag, axis=0, keepdims=True)
        rk = lax.dot_general(
            read, jnp.concatenate([key, key], axis=0), (((1,), (1,)), ((), ())),
            preferred_element_type=jnp.float32,
        )
        rk = jnp.concatenate([rk] * 4, axis=1)
        kmat = (jnp.exp(jnp.minimum(cum_j - crow, 0.0)) * causal * rk).astype(jnp.bfloat16)
        within = []
        for g in range(2):
            lanes = slice(g * 256, (g + 1) * 256)
            rhs = jnp.concatenate([driven[:, lanes]] * 4, axis=0) * bd
            within.append(dot(kmat[:, lanes], rhs))
        carried = jnp.exp(cum_j) * dot(read, state.astype(jnp.bfloat16))
        y = jnp.concatenate(within, axis=1) + carried + skip * xj
        state = jnp.exp(tot) * state + sloc_ref[0, j]
        gated = y * sg[rows]
        mean = jnp.mean(gated * gated, axis=-1, keepdims=True)
        parts.append((gated * lax.rsqrt(mean + EPS) * gain).astype(jnp.bfloat16))
    state_ref[...] = state
    normed = jnp.concatenate(parts, axis=0)

    @pl.when(strand == 0)
    def _():
        front_ref[pl.ds(pl.multiple_of(sb * ROWS, ROWS), ROWS), :] = normed

    @pl.when(strand == 1)
    def _():
        back = dot(flip_ref[...], normed).astype(jnp.bfloat16)
        start = pl.multiple_of((count - 1 - sb) * ROWS, ROWS)
        front = front_ref[pl.ds(start, ROWS), :]
        ow = ow_ref[...]
        out_ref[...] = (dot(front, ow) + dot(back, ow)).astype(out_ref.dtype)


MESH = pl.DeviceIdType.MESH
GROUP = 8


def exchange_body(
    chs, devices, rows, tokens_ref, emb_ref, iw_ref, gw_ref, sw_ref, stw_ref, ik_ref, sk_ref,
    gain_ref, ow_ref, bias_ref, decay_ref, skip_ref,
    tx_out, tst_out, tdt_out, tsg_out, ld_out, vec_out, ow_out, edge_out,
    packed, packed_all, ow_all, own, edges, small, psend, precv, osend, orecv, esend, erecv,
):
    f32, bf16 = jnp.float32, jnp.bfloat16
    seq, ch = lax.axis_index("seq"), lax.axis_index("ch")
    me = seq * chs + ch
    place = lambda d: (d // chs, lax.rem(d, chs))
    after, before = place(lax.rem(me + 1, devices)), place(lax.rem(me + devices - 1, devices))
    mate = lambda d: (seq, lax.rem(ch + d, chs))
    barrier = pltpu.get_barrier_semaphore()
    for device in [after, before] + [mate(d) for d in range(1, chs)]:
        pl.semaphore_signal(barrier, inc=1, device_id=device, device_id_type=MESH)

    wins = tokens_ref.shape[0]
    own[...] = jnp.zeros_like(own)
    own[0, :wins, :] = tokens_ref[:, pl.ds(pl.multiple_of(ch * rows, 128), 128)]
    own[1, :wins, :] = tokens_ref[:, pl.ds(pl.multiple_of(ch * rows + rows - 128, 128), 128)]
    width, heads = iw_ref.shape[1], stw_ref.shape[1]
    emb = emb_ref[...]
    packed[...] = jnp.zeros_like(packed)
    packed[0:5, :] = dot(emb, iw_ref[...]).astype(bf16).astype(f32)
    packed[8:13, :] = silu(dot(emb, gw_ref[...]).astype(bf16).astype(f32))
    pre = dot(emb, stw_ref[...])
    head = lax.broadcasted_iota(jnp.int32, (5, width), 1) // (width // heads)
    raw, rate = jnp.zeros((5, width), f32), jnp.zeros((5, width), f32)
    skip = jnp.zeros((5, width), f32)
    for h in range(heads):
        raw = jnp.where(head == h, pre[:, h : h + 1] + bias_ref[h], raw)
        rate = jnp.where(head == h, decay_ref[h], rate)
        skip = jnp.where(head == h, skip_ref[h], skip)
    step = jnp.maximum(raw, 0.0) + jnp.log1p(jnp.exp(-jnp.abs(raw)))
    packed[16:21, :] = step
    packed[24:29, :] = -step * rate
    packed[32:36, :] = ik_ref[...]
    packed[40:41, :] = skip[0:1]
    packed[41:42, :] = gain_ref[...]

    def remote(src, dst, ssem, rsem, device):
        return pltpu.make_async_remote_copy(
            src_ref=src, dst_ref=dst, send_sem=ssem, recv_sem=rsem, device_id=device,
            device_id_type=MESH,
        )

    def table_copies(d, slot):
        return (
            remote(packed, packed_all.at[slot], psend.at[d], precv.at[d], mate(d)),
            remote(ow_ref, ow_all.at[slot], osend.at[d], orecv.at[d], mate(d)),
        )

    edge_copies = (
        remote(own.at[1], edges.at[0], esend.at[0], erecv.at[0], after),
        remote(own.at[0], edges.at[1], esend.at[1], erecv.at[1], before),
    )
    pl.semaphore_wait(barrier, 1 + chs)
    for d in range(1, chs):
        for copy in table_copies(d, ch):
            copy.start()
    for copy in edge_copies:
        copy.start()
    packed_all[ch] = packed[...]
    ow_all[ch] = ow_ref[...]

    def emit(ref, table):
        hi = table.astype(bf16).astype(f32)
        mid = (table - hi).astype(bf16).astype(f32)
        low = table - hi - mid
        ref[...] = jnp.concatenate([hi, mid, low, jnp.zeros_like(hi)], axis=0).astype(bf16)

    small[...] = jnp.zeros_like(small)
    state_tab = dot(emb, sw_ref[...]).astype(bf16).astype(f32)
    for k in range(4):
        small[8 * k : 8 * k + 5, : state_tab.shape[1]] = sk_ref[k : k + 1, :] * state_tab
    emit(tst_out, small[...])
    for copy in edge_copies:
        copy.wait()
    for d in range(1, chs):
        for copy in table_copies(d, lax.rem(ch + chs - d, chs)):
            copy.wait()
    every = jnp.concatenate([packed_all[i] for i in range(chs)], axis=1)
    zeros = jnp.zeros((24, width * chs), f32)
    inner = every[0:8]
    emit(tx_out, jnp.concatenate([every[32 + k : 33 + k] * inner for k in range(4)], axis=0))
    emit(tsg_out, jnp.concatenate([every[8:16], zeros], axis=0))
    emit(tdt_out, jnp.concatenate([every[16:24], zeros], axis=0))
    emit(ld_out, jnp.concatenate([every[24:32], zeros], axis=0))
    vec_out[...] = every[40:48]
    ow_out[...] = ow_all[...]
    edge_out[...] = edges[...]


def carry_body(
    chs, groups, s_ref, out_ref, first, total, second, third, landed,
    send1, recv1, send2, recv2, send3, recv3,
):
    me = lax.axis_index("seq") * chs + lax.axis_index("ch")
    g, q = me // GROUP, lax.rem(me, GROUP)
    strand = lax.rem(q // 2, 2)
    place = lambda d: (d // chs, lax.rem(d, chs))
    mate = lambda d: place(g * GROUP + lax.rem(q + d, GROUP))
    peer = lambda d: place(lax.rem(g + d, groups) * GROUP + q)
    barrier = pltpu.get_barrier_semaphore()
    for d in range(1, GROUP):
        pl.semaphore_signal(barrier, inc=1, device_id=mate(d), device_id_type=MESH)

    def greet(d, _):
        pl.semaphore_signal(barrier, inc=1, device_id=peer(d), device_id_type=MESH)
        return 0

    lax.fori_loop(1, groups, greet, 0)
    pl.semaphore_wait(barrier, GROUP - 1 + groups - 1)

    def remote(src, dst, ssem, rsem, device):
        return pltpu.make_async_remote_copy(
            src_ref=src, dst_ref=dst, send_sem=ssem, recv_sem=rsem, device_id=device,
            device_id_type=MESH,
        )

    def within(source, target, ssem, rsem, d, slot):
        return remote(source.at[lax.rem(q + d, GROUP)], target.at[slot], ssem.at[d], rsem.at[d], mate(d))

    def swap(source, target, ssem, rsem):
        for d in range(1, GROUP):
            within(source, target, ssem, rsem, d, q).start()
        target[q] = source[q]
        for d in range(1, GROUP):
            within(source, target, ssem, rsem, d, lax.rem(q + GROUP - d, GROUP)).wait()

    swap(s_ref, first, send1, recv1)
    f32, bf16 = jnp.float32, jnp.bfloat16
    zero = jnp.zeros(out_ref.shape[1:], f32)
    member = lambda k: k + strand * (GROUP - 1 - 2 * k)
    logs = [first[member(k), 16:17, :] for k in range(GROUP)]
    grow = [jnp.exp(log) for log in logs]
    added = [first[member(k), 0:16, :] for k in range(GROUP)]
    state = zero
    for k in range(GROUP):
        state = grow[k] * state + added[k]
    total[0:16, :] = state
    total[16:24, :] = jnp.broadcast_to(sum(logs), (8, state.shape[1]))

    def across(d, slot):
        return remote(total, second.at[slot], send2.at[d], recv2.at[d], peer(d))

    def start(d, _):
        across(d, g).start()
        return 0

    def finish(d, _):
        across(d, lax.rem(g + groups - d, groups)).wait()
        return 0

    lax.fori_loop(1, groups, start, 0)
    second[g] = total[...]
    lax.fori_loop(1, groups, finish, 0)
    order = g + strand * (groups - 1 - 2 * g)

    def earlier(k, state):
        at = k + strand * (groups - 1 - 2 * k)
        new = jnp.exp(second[at, 16:17, :]) * state + second[at, 0:16, :]
        return jnp.where(k < order, new, state)

    state = lax.fori_loop(0, groups, earlier, zero)
    for k in range(GROUP):
        third[member(k)] = state.astype(bf16)
        state = grow[k] * state + added[k]
    swap(third, landed, send3, recv3)
    out_ref[...] = landed[...]


def whole_spec(array):
    return pl.BlockSpec(array.shape, lambda *_: (0,) * array.ndim)


def on_device(
    tokens, embedding, inner_weight, gate_weight, state_weight, step_weight, inner_kernel,
    state_kernel, step_bias, decay_rates, skip_gain, norm_gain, out_weight,
):
    f32, bf16 = jnp.float32, jnp.bfloat16
    wins, held = tokens.shape
    chs, seqs = lax.axis_size("ch"), lax.axis_size("seq")
    ch, seq = lax.axis_index("ch"), lax.axis_index("seq")
    rows = held // chs
    devices = seqs * chs
    me = seq * chs + ch
    heads_here = decay_rates.shape[0]
    width = inner_weight.shape[1]
    head_width = width // heads_here

    full, model = width * chs, out_weight.shape[1]
    vmem, smem = (pl.BlockSpec(memory_space=m) for m in (pltpu.VMEM, pltpu.SMEM))
    dma = pltpu.SemaphoreType.DMA
    shape = jax.ShapeDtypeStruct
    table = shape((COLS, full), bf16)
    tx, tst, tdt, tsg, ld, vec, ow, edge = pl.pallas_call(
        partial(exchange_body, chs, devices, rows),
        in_specs=[vmem] * 10 + [smem] * 3,
        out_specs=[vmem] * 8,
        out_shape=[
            table, shape((COLS, 128), bf16), table, table, table, shape((8, full), f32),
            shape((chs, width, model), bf16), shape((2, 8, 128), jnp.int32),
        ],
        scratch_shapes=[
            pltpu.VMEM((48, width), f32),
            pltpu.VMEM((chs, 48, width), f32),
            pltpu.VMEM((chs, width, model), bf16),
            pltpu.VMEM((2, 8, 128), jnp.int32),
            pltpu.VMEM((2, 8, 128), jnp.int32),
            pltpu.VMEM((32, 128), f32),
        ]
        + [dma((chs,))] * 4 + [dma((2,))] * 2,
        compiler_params=pltpu.CompilerParams(collective_id=0, has_side_effects=True),
        name="exchange",
    )(
        tokens, embedding, inner_weight, gate_weight, state_weight, step_weight, inner_kernel,
        state_kernel, norm_gain[None], out_weight, step_bias, decay_rates, skip_gain,
    )
    ow = ow.reshape(full, model)
    skip_all, gain_all = vec[0:1], vec[1:2]
    mine = lax.dynamic_slice_in_dim(tokens, ch * rows, rows, axis=1)
    none = 7
    before = jnp.where(me > 0, edge[0, :wins, 125:], none)
    after = jnp.where(me < devices - 1, edge[1, :wins, :3], none)
    mine = jnp.concatenate([before, mine, after], axis=1)
    other = jnp.where(mine < 4, 3 - mine, mine)[:, ::-1]
    ids = jnp.stack([mine, other], axis=1).reshape(wins * 2, rows + 6)
    column = np.arange(COLS)
    tap_of, id_of = (column // 8) % 4, column % 8
    onehot = jnp.zeros((wins * 2, rows, COLS), jnp.bool_)
    for k in range(4):
        tap = ids[:, 3 - k : 3 - k + rows, None] == jnp.asarray(id_of, jnp.int32)
        onehot = onehot | (tap & jnp.asarray(tap_of == k))
    onehot = onehot.astype(bf16)

    streams, steps = wins * 2, rows // ROWS
    subs = ROWS // SUB
    index = np.arange(ROWS)
    tri = jnp.asarray(
        (index[:, None] >= index[None]) & (index[:, None] // SUB == index[None] // SUB), bf16
    )
    row_spec = lambda n: pl.BlockSpec((1, ROWS, n), lambda s, b: (s, b, 0))
    x, kv, sloc, sfin = pl.pallas_call(
        state_kernel_body,
        grid=(streams, steps),
        in_specs=[row_spec(COLS)] + [whole_spec(v) for v in (tri, tx, tst, tdt, ld)],
        out_specs=[
            row_spec(full),
            row_spec(128),
            pl.BlockSpec((1, subs, 16, full), lambda s, b: (s, b, 0, 0)),
            pl.BlockSpec((2, 24, full // 2), lambda s, b: (s, 0, 0)),
        ],
        out_shape=[
            jax.ShapeDtypeStruct((streams, rows, full), bf16),
            jax.ShapeDtypeStruct((streams, rows, 128), bf16),
            jax.ShapeDtypeStruct((streams, steps * subs, 16, full), f32),
            jax.ShapeDtypeStruct((streams * 2, 24, full // 2), f32),
        ],
        scratch_shapes=[pltpu.VMEM((16, full), f32), pltpu.VMEM((1, full), f32)],
        compiler_params=pltpu.CompilerParams(vmem_limit_bytes=56 << 20),
        name="states",
    )(onehot, tri, tx, tst, tdt, ld)

    groups = devices // GROUP
    piece, message = (16, full // 2), (24, full // 2)
    incoming = pl.pallas_call(
        partial(carry_body, chs, groups),
        in_specs=[vmem],
        out_specs=vmem,
        out_shape=jax.ShapeDtypeStruct((GROUP,) + piece, bf16),
        scratch_shapes=[
            pltpu.VMEM((GROUP,) + message, f32),
            pltpu.VMEM(message, f32),
            pltpu.VMEM((groups,) + message, f32),
            pltpu.VMEM((GROUP,) + piece, bf16),
            pltpu.VMEM((GROUP,) + piece, bf16),
        ]
        + [dma((GROUP,))] * 2 + [dma((groups,))] * 2 + [dma((GROUP,))] * 2,
        compiler_params=pltpu.CompilerParams(collective_id=1, has_side_effects=True),
        name="carry",
    )(sfin)

    lane, t = np.arange(full)[None], np.arange(SUB)[:, None]
    causal = jnp.asarray(t >= lane % SUB, f32)
    diag = jnp.asarray(t == lane % SUB, f32)
    bd = jnp.asarray(np.arange(256)[:, None] // 64 == np.arange(256)[None] // 64, bf16)
    flip = jnp.asarray(np.eye(ROWS)[::-1], bf16)
    stream = lambda shape: pl.BlockSpec(
        (1,) + shape, lambda w, s, b: (w * 2 + s, b) + (0,) * (len(shape) - 1)
    )
    consts = (tri, tdt, tsg, ld, skip_all, gain_all, ow, causal, diag, bd, flip)
    out = pl.pallas_call(
        output_kernel_body,
        grid=(wins, 2, steps),
        in_specs=[
            stream((ROWS, COLS)),
            stream((ROWS, full)),
            stream((ROWS, 128)),
            stream((subs, 16, full)),
            pl.BlockSpec((2, 16, full // 2), lambda w, s, b: (w * 2 + s, 0, 0)),
        ]
        + [whole_spec(v) for v in consts],
        out_specs=pl.BlockSpec((ROWS, model), lambda w, s, b: (steps - 1 - b * s, w)),
        out_shape=jax.ShapeDtypeStruct((rows, wins * model), bf16),
        scratch_shapes=[pltpu.VMEM((16, full), f32), pltpu.VMEM((rows, full), bf16)],
        compiler_params=pltpu.CompilerParams(vmem_limit_bytes=56 << 20),
        name="outputs",
    )(onehot, x, kv, sloc, incoming, *consts)
    return out.reshape(rows, wins, model)


def solution(mesh):
    placed = (
        P(None, "seq"), P(), P(None, "ch"), P(None, "ch"), P(), P(None, "ch"), P(None, "ch"), P(),
        P("ch"), P("ch"), P("ch"), P("ch"), P("ch", None),
    )
    return jax.shard_map(
        on_device,
        mesh=mesh,
        in_specs=placed,
        out_specs=P(("seq", "ch"), None, None),
        check_vma=False,
    )
```

```python
from functools import partial

import jax
import jax.numpy as jnp
import numpy as np
from jax import lax
from jax.experimental import pallas as pl
from jax.experimental.pallas import tpu as pltpu
from jax.sharding import PartitionSpec as P

SUB = 64
ROWS = 1024
TRI = 256
EPS = 1e-05
COLS = 128


def silu(v):
    return v * (1.0 / (1.0 + jnp.exp(-v)))


def dot_t(a, b):
    return lax.dot_general(a, b, (((1,), (1,)), ((), ())), preferred_element_type=jnp.float32)


def dot(a, b):
    return jnp.dot(a, b, preferred_element_type=jnp.float32)


def logs_of(tri, oh, ld):
    counts = [dot(tri, oh[i : i + TRI]).astype(jnp.bfloat16) for i in range(0, ROWS, TRI)]
    return dot(jnp.concatenate(counts, axis=0), ld)


def state_kernel_body(ids_ref, tri_ref, tx_ref, tst_ref, tdt_ref, ld_ref, oh_ref, x_ref, kv_ref, sloc_ref, sfin_ref, state_ref, log_ref):
    @pl.when(pl.program_id(1) == 0)
    def _():
        state_ref[...] = jnp.zeros_like(state_ref)
        log_ref[...] = jnp.zeros_like(log_ref)

    ids = ids_ref[0]
    base = lax.broadcasted_iota(jnp.int32, (8, ROWS), 0)
    hits = [jnp.where(ids[k : k + 1] == base, 1.0, 0.0) for k in range(4)]
    rest = jnp.zeros((COLS - 96, ROWS), jnp.float32)
    oh = jnp.concatenate(hits * 3 + [rest], axis=0).T.astype(jnp.bfloat16)
    oh_ref[0] = oh
    x = silu(dot(oh, tx_ref[...])).astype(jnp.bfloat16)
    x_ref[0] = x
    kv = silu(dot(oh, tst_ref[...])).astype(jnp.bfloat16)
    kv_ref[0] = kv
    cum = logs_of(tri_ref[...], oh, ld_ref[...])
    dt = dot(oh, tdt_ref[...])
    state, log = state_ref[...], log_ref[...]
    for j in range(ROWS // SUB):
        rows = slice(j * SUB, (j + 1) * SUB)
        cum_j = cum[rows]
        tot = cum_j[SUB - 1 :]
        log = log + tot
        wx = (x[rows].astype(jnp.float32) * dt[rows] * jnp.exp(tot - cum_j)).astype(jnp.bfloat16)
        new = lax.dot_general(
            kv[rows, :16], wx, (((0,), (0,)), ((), ())), preferred_element_type=jnp.float32
        )
        sloc_ref[0, j] = new
        state = jnp.exp(tot) * state + new
    state_ref[...] = state
    half = state.shape[1] // 2
    log_ref[...] = log
    for i in range(2):
        lanes = slice(i * half, (i + 1) * half)
        sfin_ref[i, 0:16, :] = state[:, lanes]
        sfin_ref[i, 16:24, :] = jnp.broadcast_to(log[:, lanes], (8, half))


def output_kernel_body(
    oh_ref, x_ref, kv_ref, sloc_ref, inc_ref, tri_ref, tdt_ref, tsg_ref, ld_ref,
    skip_ref, gain_ref, ow_ref, causal_ref, diag_ref, bd_ref, flip_ref,
    out_ref, state_ref, front_ref,
):
    strand, sb = pl.program_id(1), pl.program_id(2)
    count = pl.num_programs(2)

    @pl.when(sb == 0)
    def _():
        state_ref[...] = jnp.concatenate([inc_ref[0], inc_ref[1]], axis=1).astype(jnp.float32)

    oh = oh_ref[0]
    cum = logs_of(tri_ref[...], oh, ld_ref[...])
    dt = dot(oh, tdt_ref[...])
    sg = dot(oh, tsg_ref[...])
    skip, gain = skip_ref[...], gain_ref[...]
    causal, diag, bd = causal_ref[...], diag_ref[...], bd_ref[...]
    state = state_ref[...]
    parts = []
    for j in range(ROWS // SUB):
        rows = slice(j * SUB, (j + 1) * SUB)
        cum_j = cum[rows]
        tot = cum_j[SUB - 1 :]
        xj = x_ref[0, rows, :].astype(jnp.float32)
        driven = (xj * dt[rows]).astype(jnp.bfloat16)
        key, read = kv_ref[0, rows, :16], kv_ref[0, rows, 16:32]
        crow = jnp.sum(cum_j * diag, axis=0, keepdims=True)
        rk = lax.dot_general(
            read, jnp.concatenate([key, key], axis=0), (((1,), (1,)), ((), ())),
            preferred_element_type=jnp.float32,
        )
        rk = jnp.concatenate([rk] * 4, axis=1)
        kmat = (jnp.exp(jnp.minimum(cum_j - crow, 0.0)) * causal * rk).astype(jnp.bfloat16)
        within = []
        for g in range(2):
            lanes = slice(g * 256, (g + 1) * 256)
            rhs = jnp.concatenate([driven[:, lanes]] * 4, axis=0) * bd
            within.append(dot(kmat[:, lanes], rhs))
        carried = jnp.exp(cum_j) * dot(read, state.astype(jnp.bfloat16))
        y = jnp.concatenate(within, axis=1) + carried + skip * xj
        state = jnp.exp(tot) * state + sloc_ref[0, j]
        gated = y * sg[rows]
        mean = jnp.mean(gated * gated, axis=-1, keepdims=True)
        parts.append((gated * lax.rsqrt(mean + EPS) * gain).astype(jnp.bfloat16))
    state_ref[...] = state
    normed = jnp.concatenate(parts, axis=0)

    @pl.when(strand == 0)
    def _():
        front_ref[pl.ds(pl.multiple_of(sb * ROWS, ROWS), ROWS), :] = normed

    @pl.when(strand == 1)
    def _():
        back = jnp.concatenate(
            [dot(flip_ref[...], normed[i : i + TRI]) for i in range(ROWS - TRI, -1, -TRI)], axis=0
        ).astype(jnp.bfloat16)
        start = pl.multiple_of((count - 1 - sb) * ROWS, ROWS)
        front = front_ref[pl.ds(start, ROWS), :]
        ow = ow_ref[...]
        out_ref[...] = (dot(front, ow) + dot(back, ow)).astype(out_ref.dtype)


MESH = pl.DeviceIdType.MESH
GROUP = 8


def exchange_body(
    chs, devices, rows, tokens_ref, emb_ref, iw_ref, gw_ref, sw_ref, stw_ref, ik_ref, sk_ref,
    gain_ref, ow_ref, bias_ref, decay_ref, skip_ref,
    tx_out, tst_out, tdt_out, tsg_out, ld_out, vec_out, ow_out, edge_out,
    packed, packed_all, ow_all, own, edges, small, psend, precv, osend, orecv, esend, erecv,
):
    f32, bf16 = jnp.float32, jnp.bfloat16
    seq, ch = lax.axis_index("seq"), lax.axis_index("ch")
    me = seq * chs + ch
    place = lambda d: (d // chs, lax.rem(d, chs))
    after, before = place(lax.rem(me + 1, devices)), place(lax.rem(me + devices - 1, devices))
    mate = lambda d: (seq, lax.rem(ch + d, chs))
    barrier = pltpu.get_barrier_semaphore()
    for device in [after, before] + [mate(d) for d in range(1, chs)]:
        pl.semaphore_signal(barrier, inc=1, device_id=device, device_id_type=MESH)

    wins = tokens_ref.shape[0]
    own[...] = jnp.zeros_like(own)
    own[0, :wins, :] = tokens_ref[:, pl.ds(pl.multiple_of(ch * rows, 128), 128)]
    own[1, :wins, :] = tokens_ref[:, pl.ds(pl.multiple_of(ch * rows + rows - 128, 128), 128)]
    width, heads = iw_ref.shape[1], stw_ref.shape[0]
    emb = emb_ref[...]
    packed[...] = jnp.zeros_like(packed)
    packed[0:5, :] = dot(emb, iw_ref[...]).astype(bf16).astype(f32)
    packed[8:13, :] = silu(dot(emb, gw_ref[...]).astype(bf16).astype(f32))
    pre = dot_t(emb, stw_ref[...])
    head = lax.broadcasted_iota(jnp.int32, (5, width), 1) // (width // heads)
    raw, rate = jnp.zeros((5, width), f32), jnp.zeros((5, width), f32)
    skip = jnp.zeros((5, width), f32)
    for h in range(heads):
        raw = jnp.where(head == h, pre[:, h : h + 1] + bias_ref[h], raw)
        rate = jnp.where(head == h, decay_ref[h], rate)
        skip = jnp.where(head == h, skip_ref[h], skip)
    step = jnp.maximum(raw, 0.0) + jnp.log1p(jnp.exp(-jnp.abs(raw)))
    packed[16:21, :] = step
    packed[24:29, :] = -step * rate
    packed[32:36, :] = ik_ref[...]
    packed[40:41, :] = skip[0:1]
    packed[41:42, :] = gain_ref[...]

    def remote(src, dst, ssem, rsem, device):
        return pltpu.make_async_remote_copy(
            src_ref=src, dst_ref=dst, send_sem=ssem, recv_sem=rsem, device_id=device,
            device_id_type=MESH,
        )

    def table_copies(d, slot):
        return (
            remote(packed, packed_all.at[slot], psend.at[d], precv.at[d], mate(d)),
            remote(ow_ref, ow_all.at[slot], osend.at[d], orecv.at[d], mate(d)),
        )

    edge_copies = (
        remote(own.at[1], edges.at[0], esend.at[0], erecv.at[0], after),
        remote(own.at[0], edges.at[1], esend.at[1], erecv.at[1], before),
    )
    pl.semaphore_wait(barrier, 1 + chs)
    for d in range(1, chs):
        for copy in table_copies(d, ch):
            copy.start()
    for copy in edge_copies:
        copy.start()
    packed_all[ch] = packed[...]
    ow_all[ch] = ow_ref[...]

    def emit(ref, table):
        hi = table.astype(bf16).astype(f32)
        mid = (table - hi).astype(bf16).astype(f32)
        low = table - hi - mid
        ref[...] = jnp.concatenate([hi, mid, low, jnp.zeros_like(hi)], axis=0).astype(bf16)

    small[...] = jnp.zeros_like(small)
    state_tab = dot_t(emb, sw_ref[...]).astype(bf16).astype(f32)
    for k in range(4):
        small[8 * k : 8 * k + 5, : state_tab.shape[1]] = sk_ref[k : k + 1, :] * state_tab
    emit(tst_out, small[...])
    for copy in edge_copies:
        copy.wait()
    for d in range(1, chs):
        for copy in table_copies(d, lax.rem(ch + chs - d, chs)):
            copy.wait()
    every = jnp.concatenate([packed_all[i] for i in range(chs)], axis=1)
    zeros = jnp.zeros((24, width * chs), f32)
    inner = every[0:8]
    emit(tx_out, jnp.concatenate([every[32 + k : 33 + k] * inner for k in range(4)], axis=0))
    emit(tsg_out, jnp.concatenate([every[8:16], zeros], axis=0))
    emit(tdt_out, jnp.concatenate([every[16:24], zeros], axis=0))
    emit(ld_out, jnp.concatenate([every[24:32], zeros], axis=0))
    vec_out[...] = every[40:48]
    ow_out[...] = ow_all[...]
    edge_out[...] = edges[...]


def carry_body(
    chs, groups, s_ref, out_ref, first, total, second, third, landed,
    send1, recv1, send2, recv2, send3, recv3,
):
    me = lax.axis_index("seq") * chs + lax.axis_index("ch")
    g, q = me // GROUP, lax.rem(me, GROUP)
    strand = lax.rem(q // 2, 2)
    place = lambda d: (d // chs, lax.rem(d, chs))
    mate = lambda d: place(g * GROUP + lax.rem(q + d, GROUP))
    peer = lambda d: place(lax.rem(g + d, groups) * GROUP + q)
    barrier = pltpu.get_barrier_semaphore()
    for d in range(1, GROUP):
        pl.semaphore_signal(barrier, inc=1, device_id=mate(d), device_id_type=MESH)

    def greet(d, _):
        pl.semaphore_signal(barrier, inc=1, device_id=peer(d), device_id_type=MESH)
        return 0

    lax.fori_loop(1, groups, greet, 0)
    pl.semaphore_wait(barrier, GROUP - 1 + groups - 1)

    def remote(src, dst, ssem, rsem, device):
        return pltpu.make_async_remote_copy(
            src_ref=src, dst_ref=dst, send_sem=ssem, recv_sem=rsem, device_id=device,
            device_id_type=MESH,
        )

    def within(source, target, ssem, rsem, d, slot):
        return remote(source.at[lax.rem(q + d, GROUP)], target.at[slot], ssem.at[d], rsem.at[d], mate(d))

    def swap(source, target, ssem, rsem):
        for d in range(1, GROUP):
            within(source, target, ssem, rsem, d, q).start()
        target[q] = source[q]
        for d in range(1, GROUP):
            within(source, target, ssem, rsem, d, lax.rem(q + GROUP - d, GROUP)).wait()

    swap(s_ref, first, send1, recv1)
    f32, bf16 = jnp.float32, jnp.bfloat16
    zero = jnp.zeros(out_ref.shape[1:], f32)
    member = lambda k: k + strand * (GROUP - 1 - 2 * k)
    logs = [first[member(k), 16:17, :] for k in range(GROUP)]
    grow = [jnp.exp(log) for log in logs]
    added = [first[member(k), 0:16, :] for k in range(GROUP)]
    state = zero
    for k in range(GROUP):
        state = grow[k] * state + added[k]
    total[0:16, :] = state
    total[16:24, :] = jnp.broadcast_to(sum(logs), (8, state.shape[1]))

    def across(d, slot):
        return remote(total, second.at[slot], send2.at[d], recv2.at[d], peer(d))

    def start(d, _):
        across(d, g).start()
        return 0

    def finish(d, _):
        across(d, lax.rem(g + groups - d, groups)).wait()
        return 0

    lax.fori_loop(1, groups, start, 0)
    second[g] = total[...]
    lax.fori_loop(1, groups, finish, 0)
    order = g + strand * (groups - 1 - 2 * g)

    def earlier(k, state):
        at = k + strand * (groups - 1 - 2 * k)
        new = jnp.exp(second[at, 16:17, :]) * state + second[at, 0:16, :]
        return jnp.where(k < order, new, state)

    state = lax.fori_loop(0, groups, earlier, zero)
    for k in range(GROUP):
        third[member(k)] = state.astype(bf16)
        state = grow[k] * state + added[k]
    swap(third, landed, send3, recv3)
    out_ref[...] = landed[...]


def whole_spec(array):
    return pl.BlockSpec(array.shape, lambda *_: (0,) * array.ndim)


def on_device(
    tokens, embedding, inner_weight, gate_weight, state_weight, step_weight, inner_kernel,
    state_kernel, step_bias, decay_rates, skip_gain, norm_gain, out_weight,
):
    f32, bf16 = jnp.float32, jnp.bfloat16
    wins, held = tokens.shape
    chs, seqs = lax.axis_size("ch"), lax.axis_size("seq")
    ch, seq = lax.axis_index("ch"), lax.axis_index("seq")
    rows = held // chs
    devices = seqs * chs
    me = seq * chs + ch
    heads_here = decay_rates.shape[0]
    width = inner_weight.shape[1]
    head_width = width // heads_here

    full, model = width * chs, out_weight.shape[1]
    vmem, smem = (pl.BlockSpec(memory_space=m) for m in (pltpu.VMEM, pltpu.SMEM))
    dma = pltpu.SemaphoreType.DMA
    shape = jax.ShapeDtypeStruct
    table = shape((COLS, full), bf16)
    tx, tst, tdt, tsg, ld, vec, ow, edge = pl.pallas_call(
        partial(exchange_body, chs, devices, rows),
        in_specs=[vmem] * 10 + [smem] * 3,
        out_specs=[vmem] * 8,
        out_shape=[
            table, shape((COLS, 128), bf16), table, table, table, shape((8, full), f32),
            shape((chs, width, model), bf16), shape((2, 8, 128), jnp.int32),
        ],
        scratch_shapes=[
            pltpu.VMEM((48, width), f32),
            pltpu.VMEM((chs, 48, width), f32),
            pltpu.VMEM((chs, width, model), bf16),
            pltpu.VMEM((2, 8, 128), jnp.int32),
            pltpu.VMEM((2, 8, 128), jnp.int32),
            pltpu.VMEM((32, 128), f32),
        ]
        + [dma((chs,))] * 4 + [dma((2,))] * 2,
        compiler_params=pltpu.CompilerParams(collective_id=0, has_side_effects=True),
        name="exchange",
    )(
        tokens, embedding, inner_weight, gate_weight, state_weight.T, step_weight.T, inner_kernel,
        state_kernel, norm_gain[None], out_weight, step_bias, decay_rates, skip_gain,
    )
    ow = ow.reshape(full, model)
    skip_all, gain_all = vec[0:1], vec[1:2]
    mine = lax.dynamic_slice_in_dim(tokens, ch * rows, rows, axis=1)
    none = 7
    before = jnp.where(me > 0, edge[0, :wins, 125:], none)
    after = jnp.where(me < devices - 1, edge[1, :wins, :3], none)
    mine = jnp.concatenate([before, mine, after], axis=1)
    other = jnp.where(mine < 4, 3 - mine, mine)[:, ::-1]
    ids = jnp.stack([mine, other], axis=1).reshape(wins * 2, rows + 6)
    taps = jnp.stack([ids[:, 3 - k : 3 - k + rows] for k in range(4)], axis=1)
    taps = jnp.pad(taps, ((0, 0), (0, 4), (0, 0)), constant_values=none)

    streams, steps = wins * 2, rows // ROWS
    subs = ROWS // SUB
    index = np.arange(TRI)
    tri = jnp.asarray(
        (index[:, None] >= index[None]) & (index[:, None] // SUB == index[None] // SUB), bf16
    )
    row_spec = lambda n: pl.BlockSpec((1, ROWS, n), lambda s, b: (s, b, 0))
    onehot, x, kv, sloc, sfin = pl.pallas_call(
        state_kernel_body,
        grid=(streams, steps),
        in_specs=[pl.BlockSpec((1, 8, ROWS), lambda s, b: (s, 0, b))] + [whole_spec(v) for v in (tri, tx, tst, tdt, ld)],
        out_specs=[
            row_spec(COLS),
            row_spec(full),
            row_spec(128),
            pl.BlockSpec((1, subs, 16, full), lambda s, b: (s, b, 0, 0)),
            pl.BlockSpec((2, 24, full // 2), lambda s, b: (s, 0, 0)),
        ],
        out_shape=[
            jax.ShapeDtypeStruct((streams, rows, COLS), bf16),
            jax.ShapeDtypeStruct((streams, rows, full), bf16),
            jax.ShapeDtypeStruct((streams, rows, 128), bf16),
            jax.ShapeDtypeStruct((streams, steps * subs, 16, full), f32),
            jax.ShapeDtypeStruct((streams * 2, 24, full // 2), f32),
        ],
        scratch_shapes=[pltpu.VMEM((16, full), f32), pltpu.VMEM((1, full), f32)],
        compiler_params=pltpu.CompilerParams(vmem_limit_bytes=56 << 20),
        name="states",
    )(taps, tri, tx, tst, tdt, ld)

    groups = devices // GROUP
    piece, message = (16, full // 2), (24, full // 2)
    incoming = pl.pallas_call(
        partial(carry_body, chs, groups),
        in_specs=[vmem],
        out_specs=vmem,
        out_shape=jax.ShapeDtypeStruct((GROUP,) + piece, bf16),
        scratch_shapes=[
            pltpu.VMEM((GROUP,) + message, f32),
            pltpu.VMEM(message, f32),
            pltpu.VMEM((groups,) + message, f32),
            pltpu.VMEM((GROUP,) + piece, bf16),
            pltpu.VMEM((GROUP,) + piece, bf16),
        ]
        + [dma((GROUP,))] * 2 + [dma((groups,))] * 2 + [dma((GROUP,))] * 2,
        compiler_params=pltpu.CompilerParams(collective_id=1, has_side_effects=True),
        name="carry",
    )(sfin)

    lane, t = np.arange(full)[None], np.arange(SUB)[:, None]
    causal = jnp.asarray(t >= lane % SUB, f32)
    diag = jnp.asarray(t == lane % SUB, f32)
    bd = jnp.asarray(np.arange(256)[:, None] // 64 == np.arange(256)[None] // 64, bf16)
    flip = jnp.asarray(np.eye(TRI)[::-1], bf16)
    stream = lambda shape: pl.BlockSpec(
        (1,) + shape, lambda w, s, b: (w * 2 + s, b) + (0,) * (len(shape) - 1)
    )
    consts = (tri, tdt, tsg, ld, skip_all, gain_all, ow, causal, diag, bd, flip)
    out = pl.pallas_call(
        output_kernel_body,
        grid=(wins, 2, steps),
        in_specs=[
            stream((ROWS, COLS)),
            stream((ROWS, full)),
            stream((ROWS, 128)),
            stream((subs, 16, full)),
            pl.BlockSpec((2, 16, full // 2), lambda w, s, b: (w * 2 + s, 0, 0)),
        ]
        + [whole_spec(v) for v in consts],
        out_specs=pl.BlockSpec((ROWS, model), lambda w, s, b: (steps - 1 - b * s, w)),
        out_shape=jax.ShapeDtypeStruct((rows, wins * model), bf16),
        scratch_shapes=[pltpu.VMEM((16, full), f32), pltpu.VMEM((rows, full), bf16)],
        compiler_params=pltpu.CompilerParams(vmem_limit_bytes=56 << 20),
        name="outputs",
    )(onehot, x, kv, sloc, incoming, *consts)
    return out.reshape(rows, wins, model)


def solution(mesh):
    placed = (
        P(None, "seq"), P(), P(None, "ch"), P(None, "ch"), P(), P(None, "ch"), P(None, "ch"), P(),
        P("ch"), P("ch"), P("ch"), P("ch"), P("ch", None),
    )
    return jax.shard_map(
        on_device,
        mesh=mesh,
        in_specs=placed,
        out_specs=P(("seq", "ch"), None, None),
        check_vma=False,
    )
```

```python
from functools import partial

import jax
import jax.numpy as jnp
import numpy as np
from jax import lax
from jax.experimental import pallas as pl
from jax.experimental.pallas import tpu as pltpu
from jax.sharding import PartitionSpec as P

SUB = 64
ROWS = 1024
TRI = 256
EPS = 1e-05
COLS = 128


def silu(v):
    return v * (1.0 / (1.0 + jnp.exp(-v)))


def dot_t(a, b):
    return lax.dot_general(a, b, (((1,), (1,)), ((), ())), preferred_element_type=jnp.float32)


def dot(a, b):
    return jnp.dot(a, b, preferred_element_type=jnp.float32)


def pack_log(log):
    log = jnp.broadcast_to(log, (16, log.shape[1]))
    row = lax.broadcasted_iota(jnp.int32, log.shape, 0)
    hi = log.astype(jnp.bfloat16).astype(jnp.float32)
    mid = (log - hi).astype(jnp.bfloat16).astype(jnp.float32)
    picked = jnp.where(row == 0, hi, jnp.where(row == 1, mid, log - hi - mid))
    return jnp.where(row < 3, picked, 0.0).astype(jnp.bfloat16)


def unpack_log(rows):
    return jnp.sum(rows.astype(jnp.float32), axis=0, keepdims=True)


def logs_of(tri, oh, ld):
    counts = [dot(tri, oh[i : i + TRI]).astype(jnp.bfloat16) for i in range(0, ROWS, TRI)]
    return dot(jnp.concatenate(counts, axis=0), ld)


def state_kernel_body(chs, groups, ids_ref, tri_ref, tx_ref, tst_ref, tdt_ref, ld_ref, oh_ref, x_ref, kv_ref, sloc_ref, inc_ref, state_ref, log_ref, sfin_ref, *carry):
    stream, step = pl.program_id(0), pl.program_id(1)

    @pl.when((stream == 0) & (step == 0))
    def _():
        carry_body(chs, groups, True, sfin_ref, inc_ref, *carry)

    @pl.when(pl.program_id(1) == 0)
    def _():
        state_ref[...] = jnp.zeros_like(state_ref)
        log_ref[...] = jnp.zeros_like(log_ref)

    ids = ids_ref[0]
    base = lax.broadcasted_iota(jnp.int32, (8, ROWS), 0)
    hits = [jnp.where(ids[k : k + 1] == base, 1.0, 0.0) for k in range(4)]
    rest = jnp.zeros((COLS - 96, ROWS), jnp.float32)
    oh = jnp.concatenate(hits * 3 + [rest], axis=0).T.astype(jnp.bfloat16)
    oh_ref[0] = oh
    x = silu(dot(oh, tx_ref[...])).astype(jnp.bfloat16)
    x_ref[0] = x
    kv = silu(dot(oh, tst_ref[...])).astype(jnp.bfloat16)
    kv_ref[0] = kv
    cum = logs_of(tri_ref[...], oh, ld_ref[...])
    dt = dot(oh, tdt_ref[...])
    state, log = state_ref[...], log_ref[...]
    for j in range(ROWS // SUB):
        rows = slice(j * SUB, (j + 1) * SUB)
        cum_j = cum[rows]
        tot = cum_j[SUB - 1 :]
        log = log + tot
        wx = (x[rows].astype(jnp.float32) * dt[rows] * jnp.exp(tot - cum_j)).astype(jnp.bfloat16)
        new = lax.dot_general(
            kv[rows, :16], wx, (((0,), (0,)), ((), ())), preferred_element_type=jnp.float32
        )
        sloc_ref[0, j] = new
        state = jnp.exp(tot) * state + new
    state_ref[...] = state
    half = state.shape[1] // 2
    log_ref[...] = log
    for i in range(2):
        lanes = slice(i * half, (i + 1) * half)
        sfin_ref[stream * 2 + i, 0:16, :] = state[:, lanes].astype(jnp.bfloat16)
        sfin_ref[stream * 2 + i, 16:32, :] = pack_log(log[:, lanes])

    @pl.when((stream == pl.num_programs(0) - 1) & (step == pl.num_programs(1) - 1))
    def _():
        carry_body(chs, groups, False, sfin_ref, inc_ref, *carry)


def output_kernel_body(
    oh_ref, x_ref, kv_ref, sloc_ref, inc_ref, tri_ref, tdt_ref, tsg_ref, ld_ref,
    skip_ref, gain_ref, ow_ref, causal_ref, diag_ref, bd_ref, flip_ref,
    out_ref, state_ref, front_ref,
):
    strand, sb = pl.program_id(1), pl.program_id(2)
    count = pl.num_programs(2)

    @pl.when(sb == 0)
    def _():
        state_ref[...] = jnp.concatenate([inc_ref[0], inc_ref[1]], axis=1).astype(jnp.float32)

    oh = oh_ref[0]
    cum = logs_of(tri_ref[...], oh, ld_ref[...])
    dt = dot(oh, tdt_ref[...])
    sg = dot(oh, tsg_ref[...])
    skip, gain = skip_ref[...], gain_ref[...]
    causal, diag, bd = causal_ref[...], diag_ref[...], bd_ref[...]
    state = state_ref[...]
    parts = []
    for j in range(ROWS // SUB):
        rows = slice(j * SUB, (j + 1) * SUB)
        cum_j = cum[rows]
        tot = cum_j[SUB - 1 :]
        xj = x_ref[0, rows, :].astype(jnp.float32)
        driven = (xj * dt[rows]).astype(jnp.bfloat16)
        key, read = kv_ref[0, rows, :16], kv_ref[0, rows, 16:32]
        crow = jnp.sum(cum_j * diag, axis=0, keepdims=True)
        rk = lax.dot_general(
            read, jnp.concatenate([key, key], axis=0), (((1,), (1,)), ((), ())),
            preferred_element_type=jnp.float32,
        )
        rk = jnp.concatenate([rk] * 4, axis=1)
        kmat = (jnp.exp(jnp.minimum(cum_j - crow, 0.0)) * causal * rk).astype(jnp.bfloat16)
        within = []
        for g in range(2):
            lanes = slice(g * 256, (g + 1) * 256)
            rhs = jnp.concatenate([driven[:, lanes]] * 4, axis=0) * bd
            within.append(dot(kmat[:, lanes], rhs))
        carried = jnp.exp(cum_j) * dot(read, state.astype(jnp.bfloat16))
        y = jnp.concatenate(within, axis=1) + carried + skip * xj
        state = jnp.exp(tot) * state + sloc_ref[0, j]
        gated = y * sg[rows]
        mean = jnp.mean(gated * gated, axis=-1, keepdims=True)
        parts.append((gated * lax.rsqrt(mean + EPS) * gain).astype(jnp.bfloat16))
    state_ref[...] = state
    normed = jnp.concatenate(parts, axis=0)

    @pl.when(strand == 0)
    def _():
        front_ref[pl.ds(pl.multiple_of(sb * ROWS, ROWS), ROWS), :] = normed

    @pl.when(strand == 1)
    def _():
        back = jnp.concatenate(
            [dot(flip_ref[...], normed[i : i + TRI]) for i in range(ROWS - TRI, -1, -TRI)], axis=0
        ).astype(jnp.bfloat16)
        start = pl.multiple_of((count - 1 - sb) * ROWS, ROWS)
        front = front_ref[pl.ds(start, ROWS), :]
        ow = ow_ref[...]
        out_ref[...] = (dot(front, ow) + dot(back, ow)).astype(out_ref.dtype)


MESH = pl.DeviceIdType.MESH
GROUP = 8


def exchange_body(
    chs, devices, rows, tokens_ref, emb_ref, iw_ref, gw_ref, sw_ref, stw_ref, ik_ref, sk_ref,
    gain_ref, ow_ref, bias_ref, decay_ref, skip_ref,
    tx_out, tst_out, tdt_out, tsg_out, ld_out, vec_out, ow_out, edge_out,
    packed, packed_all, ow_all, own, edges, small, psend, precv, osend, orecv, esend, erecv,
):
    f32, bf16 = jnp.float32, jnp.bfloat16
    seq, ch = lax.axis_index("seq"), lax.axis_index("ch")
    me = seq * chs + ch
    place = lambda d: (d // chs, lax.rem(d, chs))
    after, before = place(lax.rem(me + 1, devices)), place(lax.rem(me + devices - 1, devices))
    mate = lambda d: (seq, lax.rem(ch + d, chs))
    barrier = pltpu.get_barrier_semaphore()
    for device in [after, before] + [mate(d) for d in range(1, chs)]:
        pl.semaphore_signal(barrier, inc=1, device_id=device, device_id_type=MESH)

    wins = tokens_ref.shape[0]
    own[...] = jnp.zeros_like(own)
    own[0, :wins, :] = tokens_ref[:, pl.ds(pl.multiple_of(ch * rows, 128), 128)]
    own[1, :wins, :] = tokens_ref[:, pl.ds(pl.multiple_of(ch * rows + rows - 128, 128), 128)]
    def remote(src, dst, ssem, rsem, device):
        return pltpu.make_async_remote_copy(
            src_ref=src, dst_ref=dst, send_sem=ssem, recv_sem=rsem, device_id=device,
            device_id_type=MESH,
        )

    def table_copies(d, slot):
        return (
            remote(packed, packed_all.at[slot], psend.at[d], precv.at[d], mate(d)),
            remote(ow_ref, ow_all.at[slot], osend.at[d], orecv.at[d], mate(d)),
        )

    edge_copies = (
        remote(own.at[1], edges.at[0], esend.at[0], erecv.at[0], after),
        remote(own.at[0], edges.at[1], esend.at[1], erecv.at[1], before),
    )
    pl.semaphore_wait(barrier, 1 + chs)
    for copy in edge_copies:
        copy.start()
    for d in range(1, chs):
        table_copies(d, ch)[1].start()
    width, heads = iw_ref.shape[1], stw_ref.shape[0]
    emb = emb_ref[...]
    packed[...] = jnp.zeros_like(packed)
    packed[0:5, :] = dot(emb, iw_ref[...]).astype(bf16).astype(f32)
    packed[8:13, :] = silu(dot(emb, gw_ref[...]).astype(bf16).astype(f32))
    pre = dot_t(emb, stw_ref[...])
    head = lax.broadcasted_iota(jnp.int32, (5, width), 1) // (width // heads)
    raw, rate = jnp.zeros((5, width), f32), jnp.zeros((5, width), f32)
    skip = jnp.zeros((5, width), f32)
    for h in range(heads):
        raw = jnp.where(head == h, pre[:, h : h + 1] + bias_ref[h], raw)
        rate = jnp.where(head == h, decay_ref[h], rate)
        skip = jnp.where(head == h, skip_ref[h], skip)
    step = jnp.maximum(raw, 0.0) + jnp.log1p(jnp.exp(-jnp.abs(raw)))
    packed[16:21, :] = step
    packed[24:29, :] = -step * rate
    packed[32:36, :] = ik_ref[...]
    packed[40:41, :] = skip[0:1]
    packed[41:42, :] = gain_ref[...]

    for d in range(1, chs):
        table_copies(d, ch)[0].start()
    packed_all[ch] = packed[...]
    ow_all[ch] = ow_ref[...]

    def emit(ref, table):
        hi = table.astype(bf16).astype(f32)
        mid = (table - hi).astype(bf16).astype(f32)
        low = table - hi - mid
        ref[...] = jnp.concatenate([hi, mid, low, jnp.zeros_like(hi)], axis=0).astype(bf16)

    small[...] = jnp.zeros_like(small)
    state_tab = dot_t(emb, sw_ref[...]).astype(bf16).astype(f32)
    for k in range(4):
        small[8 * k : 8 * k + 5, : state_tab.shape[1]] = sk_ref[k : k + 1, :] * state_tab
    emit(tst_out, small[...])
    for copy in edge_copies:
        copy.wait()
    for d in range(1, chs):
        for copy in table_copies(d, lax.rem(ch + chs - d, chs)):
            copy.wait()
    every = jnp.concatenate([packed_all[i] for i in range(chs)], axis=1)
    zeros = jnp.zeros((24, width * chs), f32)
    inner = every[0:8]
    emit(tx_out, jnp.concatenate([every[32 + k : 33 + k] * inner for k in range(4)], axis=0))
    emit(tsg_out, jnp.concatenate([every[8:16], zeros], axis=0))
    emit(tdt_out, jnp.concatenate([every[16:24], zeros], axis=0))
    emit(ld_out, jnp.concatenate([every[24:32], zeros], axis=0))
    vec_out[...] = every[40:48]
    ow_out[...] = ow_all[...]
    edge_out[...] = edges[...]


def carry_body(
    chs, groups, opening, s_ref, out_ref, first, total, second, third, landed,
    send1, recv1, send2, recv2, send3, recv3,
):
    me = lax.axis_index("seq") * chs + lax.axis_index("ch")
    g, q = me // GROUP, lax.rem(me, GROUP)
    strand = lax.rem(q // 2, 2)
    place = lambda d: (d // chs, lax.rem(d, chs))
    mate = lambda d: place(g * GROUP + lax.rem(q + d, GROUP))
    peer = lambda d: place(lax.rem(g + d, groups) * GROUP + q)
    barrier = pltpu.get_barrier_semaphore()

    def greet(d, _):
        pl.semaphore_signal(barrier, inc=1, device_id=peer(d), device_id_type=MESH)
        return 0

    if opening:
        for d in range(1, GROUP):
            pl.semaphore_signal(barrier, inc=1, device_id=mate(d), device_id_type=MESH)
        lax.fori_loop(1, groups, greet, 0)
        return
    pl.semaphore_wait(barrier, GROUP - 1 + groups - 1)

    def remote(src, dst, ssem, rsem, device):
        return pltpu.make_async_remote_copy(
            src_ref=src, dst_ref=dst, send_sem=ssem, recv_sem=rsem, device_id=device,
            device_id_type=MESH,
        )

    def within(source, target, ssem, rsem, d, slot):
        return remote(source.at[lax.rem(q + d, GROUP)], target.at[slot], ssem.at[d], rsem.at[d], mate(d))

    def swap(source, target, ssem, rsem):
        for d in range(1, GROUP):
            within(source, target, ssem, rsem, d, q).start()
        target[q] = source[q]
        for d in range(1, GROUP):
            within(source, target, ssem, rsem, d, lax.rem(q + GROUP - d, GROUP)).wait()

    swap(s_ref, first, send1, recv1)
    f32, bf16 = jnp.float32, jnp.bfloat16
    zero = jnp.zeros(out_ref.shape[1:], f32)
    member = lambda k: k + strand * (GROUP - 1 - 2 * k)
    logs = [unpack_log(first[member(k), 16:32, :]) for k in range(GROUP)]
    grow = [jnp.exp(log) for log in logs]
    added = [first[member(k), 0:16, :].astype(f32) for k in range(GROUP)]
    state = zero
    for k in range(GROUP):
        state = grow[k] * state + added[k]
    total[0:16, :] = state.astype(bf16)
    total[16:32, :] = pack_log(sum(logs))

    def across(d, slot):
        return remote(total, second.at[slot], send2.at[d], recv2.at[d], peer(d))

    def start(d, _):
        across(d, g).start()
        return 0

    def finish(d, _):
        across(d, lax.rem(g + groups - d, groups)).wait()
        return 0

    lax.fori_loop(1, groups, start, 0)
    second[g] = total[...]
    lax.fori_loop(1, groups, finish, 0)
    order = g + strand * (groups - 1 - 2 * g)

    def earlier(k, state):
        at = k + strand * (groups - 1 - 2 * k)
        new = jnp.exp(unpack_log(second[at, 16:32, :])) * state + second[at, 0:16, :].astype(f32)
        return jnp.where(k < order, new, state)

    state = lax.fori_loop(0, groups, earlier, zero)
    for k in range(GROUP):
        third[member(k)] = state.astype(bf16)
        state = grow[k] * state + added[k]
    swap(third, landed, send3, recv3)
    out_ref[...] = landed[...]


def whole_spec(array):
    return pl.BlockSpec(array.shape, lambda *_: (0,) * array.ndim)


def on_device(
    tokens, embedding, inner_weight, gate_weight, state_weight, step_weight, inner_kernel,
    state_kernel, step_bias, decay_rates, skip_gain, norm_gain, out_weight,
):
    f32, bf16 = jnp.float32, jnp.bfloat16
    wins, held = tokens.shape
    chs, seqs = lax.axis_size("ch"), lax.axis_size("seq")
    ch, seq = lax.axis_index("ch"), lax.axis_index("seq")
    rows = held // chs
    devices = seqs * chs
    me = seq * chs + ch
    heads_here = decay_rates.shape[0]
    width = inner_weight.shape[1]
    head_width = width // heads_here

    full, model = width * chs, out_weight.shape[1]
    vmem, smem = (pl.BlockSpec(memory_space=m) for m in (pltpu.VMEM, pltpu.SMEM))
    dma = pltpu.SemaphoreType.DMA
    shape = jax.ShapeDtypeStruct
    table = shape((COLS, full), bf16)
    tx, tst, tdt, tsg, ld, vec, ow, edge = pl.pallas_call(
        partial(exchange_body, chs, devices, rows),
        in_specs=[vmem] * 10 + [smem] * 3,
        out_specs=[vmem] * 8,
        out_shape=[
            table, shape((COLS, 128), bf16), table, table, table, shape((8, full), f32),
            shape((chs, width, model), bf16), shape((2, 8, 128), jnp.int32),
        ],
        scratch_shapes=[
            pltpu.VMEM((48, width), f32),
            pltpu.VMEM((chs, 48, width), f32),
            pltpu.VMEM((chs, width, model), bf16),
            pltpu.VMEM((2, 8, 128), jnp.int32),
            pltpu.VMEM((2, 8, 128), jnp.int32),
            pltpu.VMEM((32, 128), f32),
        ]
        + [dma((chs,))] * 4 + [dma((2,))] * 2,
        compiler_params=pltpu.CompilerParams(collective_id=0, has_side_effects=True),
        name="exchange",
    )(
        tokens, embedding, inner_weight, gate_weight, state_weight.T, step_weight.T, inner_kernel,
        state_kernel, norm_gain[None], out_weight, step_bias, decay_rates, skip_gain,
    )
    ow = ow.reshape(full, model)
    skip_all, gain_all = vec[0:1], vec[1:2]
    mine = lax.dynamic_slice_in_dim(tokens, ch * rows, rows, axis=1)
    none = 7
    before = jnp.where(me > 0, edge[0, :wins, 125:], none)
    after = jnp.where(me < devices - 1, edge[1, :wins, :3], none)
    mine = jnp.concatenate([before, mine, after], axis=1)
    other = jnp.where(mine < 4, 3 - mine, mine)[:, ::-1]
    ids = jnp.stack([mine, other], axis=1).reshape(wins * 2, rows + 6)
    taps = jnp.stack([ids[:, 3 - k : 3 - k + rows] for k in range(4)], axis=1)
    taps = jnp.pad(taps, ((0, 0), (0, 4), (0, 0)), constant_values=none)

    streams, steps = wins * 2, rows // ROWS
    subs = ROWS // SUB
    index = np.arange(TRI)
    tri = jnp.asarray(
        (index[:, None] >= index[None]) & (index[:, None] // SUB == index[None] // SUB), bf16
    )
    row_spec = lambda n: pl.BlockSpec((1, ROWS, n), lambda s, b: (s, b, 0))
    groups = devices // GROUP
    piece, message = (16, full // 2), (32, full // 2)
    onehot, x, kv, sloc, incoming = pl.pallas_call(
        partial(state_kernel_body, chs, groups),
        grid=(streams, steps),
        in_specs=[pl.BlockSpec((1, 8, ROWS), lambda s, b: (s, 0, b))] + [whole_spec(v) for v in (tri, tx, tst, tdt, ld)],
        out_specs=[
            row_spec(COLS),
            row_spec(full),
            row_spec(128),
            pl.BlockSpec((1, subs, 16, full), lambda s, b: (s, b, 0, 0)),
            pl.BlockSpec((GROUP,) + piece, lambda s, b: (0, 0, 0)),
        ],
        out_shape=[
            jax.ShapeDtypeStruct((streams, rows, COLS), bf16),
            jax.ShapeDtypeStruct((streams, rows, full), bf16),
            jax.ShapeDtypeStruct((streams, rows, 128), bf16),
            jax.ShapeDtypeStruct((streams, steps * subs, 16, full), f32),
            jax.ShapeDtypeStruct((GROUP,) + piece, bf16),
        ],
        scratch_shapes=[
            pltpu.VMEM((16, full), f32),
            pltpu.VMEM((1, full), f32),
            pltpu.VMEM((GROUP,) + message, bf16),
            pltpu.VMEM((GROUP,) + message, bf16),
            pltpu.VMEM(message, bf16),
            pltpu.VMEM((groups,) + message, bf16),
            pltpu.VMEM((GROUP,) + piece, bf16),
            pltpu.VMEM((GROUP,) + piece, bf16),
        ]
        + [dma((GROUP,))] * 2 + [dma((groups,))] * 2 + [dma((GROUP,))] * 2,
        compiler_params=pltpu.CompilerParams(
            vmem_limit_bytes=56 << 20, collective_id=1, has_side_effects=True
        ),
        name="states",
    )(taps, tri, tx, tst, tdt, ld)

    lane, t = np.arange(full)[None], np.arange(SUB)[:, None]
    causal = jnp.asarray(t >= lane % SUB, f32)
    diag = jnp.asarray(t == lane % SUB, f32)
    bd = jnp.asarray(np.arange(256)[:, None] // 64 == np.arange(256)[None] // 64, bf16)
    flip = jnp.asarray(np.eye(TRI)[::-1], bf16)
    stream = lambda shape: pl.BlockSpec(
        (1,) + shape, lambda w, s, b: (w * 2 + s, b) + (0,) * (len(shape) - 1)
    )
    consts = (tri, tdt, tsg, ld, skip_all, gain_all, ow, causal, diag, bd, flip)
    out = pl.pallas_call(
        output_kernel_body,
        grid=(wins, 2, steps),
        in_specs=[
            stream((ROWS, COLS)),
            stream((ROWS, full)),
            stream((ROWS, 128)),
            stream((subs, 16, full)),
            pl.BlockSpec((2, 16, full // 2), lambda w, s, b: (w * 2 + s, 0, 0)),
        ]
        + [whole_spec(v) for v in consts],
        out_specs=pl.BlockSpec((ROWS, model), lambda w, s, b: (steps - 1 - b * s, w)),
        out_shape=jax.ShapeDtypeStruct((rows, wins * model), bf16),
        scratch_shapes=[pltpu.VMEM((16, full), f32), pltpu.VMEM((rows, full), bf16)],
        compiler_params=pltpu.CompilerParams(vmem_limit_bytes=56 << 20),
        name="outputs",
    )(onehot, x, kv, sloc, incoming, *consts)
    return out.reshape(rows, wins, model)


def solution(mesh):
    placed = (
        P(None, "seq"), P(), P(None, "ch"), P(None, "ch"), P(), P(None, "ch"), P(None, "ch"), P(),
        P("ch"), P("ch"), P("ch"), P("ch"), P("ch", None),
    )
    return jax.shard_map(
        on_device,
        mesh=mesh,
        in_specs=placed,
        out_specs=P(("seq", "ch"), None, None),
        check_vma=False,
    )
```
